32 devices in a mesh: gx: 4 (over z), gy: 4 (over x, core), gz: 2 (over y).
Axes of the slice: x: 2, y: 2, z: 4, core: 2. Of those that a mesh axis runs over, the one named last changes fastest.
Arguments:
- basis: bfloat16 [224, 64, 4096], P(('gx', 'gy', 'gz')), may hold values from -6 to 6
- density_blocks: bfloat16 [1536, 4096], P(('gx', 'gy', 'gz')), may hold values from -0.014953613 to 0.014953613
- pair_groups: int32 [2, 1536], P(None, ('gx', 'gy', 'gz')), may hold values from 0 to 6, as said below
- owner: int32 [1536, 1], P(('gx', 'gy', 'gz')), may hold values from 0 to 15; in each aligned block of 48 rows (0 to 47, 48 to 95, ...) at most 6 rows name the same one
- owner_slot: int32 [1536], P(('gx', 'gy', 'gz')), may hold values from 0 to 47
Outputs:
- ks_blocks: bfloat16 [1536, 4096], P(('gx', 'gy', 'gz'))
- xc_potential: float32 [32, 32, 16], P('gx', 'gy', 'gz')
The draws below stay inside these ranges and needn't reach their ends.
Inputs may be any that keep to these rules, and one draw needn't show every extreme that they name: At most 6 pairs of one subdomain name the same owner, and in every draw some subdomain's pairs name one owner exactly 6 times; every owner is named by some pair. `pair_groups`: the pairs of one subdomain are distinct ordered pairs of its groups.
All inputs are finite; a program needn't handle non-finite values.
Results may differ from the reference program's by a relative error of at most 0.0055.
Values may be sent and summed in bfloat16 or wider, within the bound.
No kernel may reach another device: no remote copies, remote signals or barrier semaphores. Data moves between devices by JAX's collectives and lax.ppermute only.
A program may use at most 64 MiB of HBM per device.

```python
import math
import jax
import jax.numpy as jnp
import numpy as np
from jax import lax

BASIS = 64
GROUPS_DEV = 7
PAIRS_DEV = 48
CELLS = 8
RIM = 4
EXT = 16
EXT3 = 4096
NX = 32
NY = 32
NZ = 16
OWNERS = 16
CAP = 6
BLK_DEV = 48
GROUPS = 224
PAIRS = 1536
BLOCKS = 1536
N_GX = 4
N_GY = 4
N_GZ = 2


def draw_pair_groups(key, part):
    device_count = PAIRS // PAIRS_DEV
    keys = jax.random.split(jax.random.fold_in(key, 17), device_count)

    def one_device(device_key):
        return jax.random.permutation(device_key, GROUPS_DEV * GROUPS_DEV)[:PAIRS_DEV]
    pair_codes = jax.vmap(one_device)(keys).reshape(-1).astype(jnp.int32)
    return jnp.stack([pair_codes // GROUPS_DEV, pair_codes % GROUPS_DEV]).astype(jnp.int32)


def set_ends(result, rng, smallest, high):
    shape = result.shape
    spot = [jax.random.randint(jax.random.fold_in(rng, axis), (), 0, shape[axis]) for axis in range(len(shape))]
    result = result.at[tuple(spot)].set(smallest)
    longest = shape.index(max(shape))
    spot[longest] = (spot[longest] + 1) % shape[longest]
    return result.at[tuple(spot)].set(high)


def levels(key, shape, pieces, low, high):
    factor_of, own = 1.0, jax.random.fold_in(key, 6)
    for dim, shards_of in pieces:
        heights = jnp.exp(jax.random.uniform(jax.random.fold_in(own, dim), (shards_of,), jnp.float32, low / len(pieces), high / len(pieces)))
        factor_of = factor_of * jnp.repeat(heights, shape[dim] // shards_of).reshape([-1 if axis == dim else 1 for axis in range(len(shape))])
    return factor_of


def routed_block(rng, own, number, rows, number_of, top, most, skew):
    sequence = jax.random.permutation(rng, number_of)
    heavy_load, common = load_shares(number_of, rows * top, most, skew, True), load_shares(number_of, rows * top, most, skew, False)
    places = jnp.arange(number_of)

    def named(sizes, turn):
        used = int((sizes > 0).sum())
        fixed = max(1, used // 4)
        passed = fixed + (places - fixed + turn * (used - fixed)) % max(1, number_of - fixed)
        return jnp.zeros((number_of,), jnp.int32).at[sequence[jnp.where(places < fixed, places, passed)]].set(jnp.asarray(sizes, jnp.int32))

    sizes = jnp.where(number % 4 == 0, named(heavy_load, number // 4), named(common, number - number // 4 - 1))
    mixed = jax.random.permutation(jax.random.fold_in(own, 3), number_of)
    source_of, receiver = mixed[0:number_of // 2 * 2:2], mixed[1:number_of // 2 * 2:2]
    margin = jnp.minimum(sizes[source_of] - 1, most - sizes[receiver]) // 2
    margin = jnp.where((source_of == sequence[0]) | (receiver == sequence[0]) | (sizes[receiver] == 0), 0, jnp.maximum(margin, 0))
    passed = jax.random.randint(jax.random.fold_in(own, 4), (number_of // 2,), 0, 1 << 20) % (margin + 1)
    sizes = sizes.at[source_of].add(-passed).at[receiver].add(passed)
    items = jnp.searchsorted(jnp.cumsum(sizes), jnp.arange(rows * top), side="right").astype(jnp.int32)
    grid = items.reshape(top, rows).T
    grid = grid[jax.random.permutation(jax.random.fold_in(own, 1), rows)]
    turn = jax.random.randint(jax.random.fold_in(own, 2), (rows, 1), 0, top)
    return jnp.take_along_axis(grid, (jnp.arange(top)[None, :] + turn) % top, axis=1)


def load_shares(number_of, total, bound, lean, full):
    portions = [(1 << 20) // math.isqrt(standing ** lean) + 1 for standing in range(1, number_of + 1)]
    largest = bound if full else min(bound, max(-(-total // number_of), total * portions[0] // sum(portions)))
    least = 1 if total - largest >= number_of - 1 else 0
    holding, rest = [largest] + [least] * (number_of - 1), total - largest - least * (number_of - 1)
    while rest > 0:
        movable = [i for i in range(1, number_of) if holding[i] < largest] or [i for i in range(1, number_of) if holding[i] < bound]
        mass, left = sum([portions[i] for i in movable]), rest
        for i in movable:
            extra = min(bound - holding[i], max(1, left * portions[i] // mass), rest)
            holding[i] = holding[i] + extra
            rest = rest - extra
    return np.array(holding)


def noise(rng, dims, deviation, limit, shards=(), kind=jnp.bfloat16):
    entries = jax.random.normal(rng, dims, jnp.float32) * deviation
    if len(shards) > 0:
        entries = levels(rng, dims, shards, -0.22, 0.18) * entries
    return jnp.clip(entries, min=-limit, max=limit).astype(kind)


def setup_inputs(seed: int = 0) -> dict:
    streams_of = jax.random.split(jax.random.key(seed), 6)
    basis = noise(streams_of[0], (GROUPS, BASIS, EXT3), 1.0, 6.0, ((0, 32),))
    density_blocks = noise(streams_of[1], (PAIRS, BASIS * BASIS), 0.0025, 0.014953613, ((0, 32),))
    pair_groups = draw_pair_groups(jax.random.fold_in(streams_of[5], 71), 0)
    owner_keys = jax.random.split(jax.random.fold_in(streams_of[3], 1), PAIRS // PAIRS_DEV)
    owner_turns = jax.random.permutation(jax.random.fold_in(streams_of[3], 3), PAIRS // PAIRS_DEV)
    owner = jax.vmap(lambda own, number: routed_block(jax.random.fold_in(streams_of[3], 2), own, number, PAIRS_DEV, OWNERS, 1, CAP, 2))(owner_keys, owner_turns).reshape((PAIRS, 1))
    owner_slot = set_ends(jax.random.randint(streams_of[4], (PAIRS,), 0, BLK_DEV), jax.random.fold_in(streams_of[4], 1), 0, BLK_DEV - 1).astype(jnp.int32)
    return dict(basis=basis, density_blocks=density_blocks, pair_groups=pair_groups, owner=owner, owner_slot=owner_slot)


XC_COEF = 0.9847450218426965
GRID_WEIGHT = 0.015625


def slater_potential(density):
    return -XC_COEF * density / jnp.cbrt(density * density + 1.0)


def reference(basis, density_blocks, pair_groups, owner, owner_slot):
    devices = N_GX * N_GY * N_GZ
    basis_dev = basis.reshape(devices, GROUPS_DEV, BASIS, EXT3)
    blocks_dev = density_blocks.reshape(devices, PAIRS_DEV, BASIS, BASIS)
    first_group = pair_groups[0].reshape(devices, PAIRS_DEV)
    second_group = pair_groups[1].reshape(devices, PAIRS_DEV)

    def collocate(inputs):
        tables, blocks, left_index, right_index = inputs
        tables32 = tables.astype(jnp.float32)
        right_image = jnp.einsum("pmn,pnr->pmr", blocks.astype(jnp.float32), tables32[right_index])
        return jnp.sum(tables32[left_index] * right_image, axis=(0, 1))

    box_density = lax.map(collocate, (basis_dev, blocks_dev, first_group, second_group))
    device_ids = jnp.arange(devices, dtype=jnp.int32)
    plane_x = device_ids // (N_GY * N_GZ)
    plane_y = (device_ids // N_GZ) % N_GY
    plane_z = device_ids % N_GZ
    offsets = jnp.arange(EXT, dtype=jnp.int32) - RIM
    cell_x = (plane_x[:, None] * CELLS + offsets[None, :]) % NX
    cell_y = (plane_y[:, None] * CELLS + offsets[None, :]) % NY
    cell_z = (plane_z[:, None] * CELLS + offsets[None, :]) % NZ
    flat_cells = (cell_x[:, :, None, None] * (NY * NZ) + cell_y[:, None, :, None] * NZ + cell_z[:, None, None, :]).reshape(devices, EXT3).astype(jnp.int32)
    density = jnp.zeros((NX * NY * NZ,), jnp.float32).at[flat_cells.reshape(-1)].add(box_density.reshape(-1))
    potential = slater_potential(density)
    potential_ext = potential[flat_cells]

    def integrate(inputs):
        tables, local_potential, left_index, right_index = inputs
        tables32 = tables.astype(jnp.float32)
        weighted = (tables32 * local_potential[None, None, :]).astype(jnp.bfloat16)
        weighted = lax.optimization_barrier(weighted).astype(jnp.float32)
        blocks = jnp.einsum("pmr,pnr->pmn", weighted[left_index], tables32[right_index]) * GRID_WEIGHT
        return blocks.astype(jnp.bfloat16).reshape(PAIRS_DEV, BASIS * BASIS)

    pair_blocks = lax.map(integrate, (basis_dev, potential_ext, first_group, second_group))
    owner_dev = owner.reshape(devices, PAIRS_DEV) * N_GZ + plane_z[:, None]
    target_rows = (owner_dev * BLK_DEV + owner_slot.reshape(devices, PAIRS_DEV)).astype(jnp.int32)
    ks_blocks = jnp.zeros((BLOCKS, BASIS * BASIS), jnp.float32).at[target_rows.reshape(-1)].add(pair_blocks.reshape(-1, BASIS * BASIS).astype(jnp.float32))
    return ks_blocks.astype(jnp.bfloat16), potential.reshape(NX, NY, NZ)
```

```python
import jax
import jax.numpy as jnp
from jax import lax
from jax.sharding import PartitionSpec as P

BASIS = 64
CELLS = 8
RIM = 4
EXT = 16
EXT3 = 4096
LANES = 128

XC_COEF = 0.9847450218426965
GRID_WEIGHT = 0.015625


def slater_potential(density):
    return -XC_COEF * density / jnp.cbrt(density * density + 1.0)


def neighbour_swaps(count, first):
    pairs = []
    for low in range(first, count + first, 2):
        left, right = low % count, (low + 1) % count
        pairs += [(left, right), (right, left)]
    return pairs


def merged(low, high, axis, forward=False):
    count = lax.axis_size(axis)
    if count == 2:
        got = lax.ppermute(jnp.stack([high, low]), axis, neighbour_swaps(count, 0))
        return low + got[0], high + got[1]
    odd = lax.axis_index(axis) % 2 == 1
    near, far = jnp.where(odd, low, high), jnp.where(odd, high, low)
    if forward and count == 4:
        got = lax.ppermute(jnp.stack([near, far]), axis, neighbour_swaps(count, 0))
        near = near + got[0]
        far = far + lax.ppermute(got[1], axis, [(i, i ^ 2) for i in range(count)])
    else:
        got = lax.ppermute(near, axis, neighbour_swaps(count, 0))
        other = lax.ppermute(far, axis, neighbour_swaps(count, 1))
        near, far = near + got, far + other
    return jnp.where(odd, near, far), jnp.where(odd, far, near)


def z_halves_swapped(box):
    lane = lax.broadcasted_iota(jnp.int32, box.shape, box.ndim - 1)
    return jnp.where(
        lane % EXT < EXT // 2,
        jnp.roll(box, -EXT // 2, axis=-1),
        jnp.roll(box, EXT // 2, axis=-1),
    )


def merged_z(box, axis):
    count = lax.axis_size(axis)
    swapped = z_halves_swapped(box)
    if count == 2:
        return box + lax.ppermute(swapped, axis, neighbour_swaps(count, 0))
    odd = lax.axis_index(axis) % 2 == 1
    lane = lax.broadcasted_iota(jnp.int32, box.shape, box.ndim - 1)
    in_high = lane % EXT >= EXT // 2
    first = lax.ppermute(swapped, axis, neighbour_swaps(count, 0))
    second = lax.ppermute(swapped, axis, neighbour_swaps(count, 1))
    return box + jnp.where(in_high != odd, first, second)


def per_device(basis, density_blocks, pair_groups, owner, owner_slot):
    groups = basis.shape[0]
    pairs = density_blocks.shape[0]
    square = BASIS * BASIS
    pair_codes = pair_groups[0] * groups + pair_groups[1]
    code_match = (
        pair_codes[:, None] == jnp.arange(groups * groups, dtype=jnp.int32)[None, :]
    ).astype(jnp.bfloat16)
    dense_blocks = lax.dot_general(
        code_match, density_blocks, (((0,), (0,)), ((), ())), preferred_element_type=jnp.float32
    ).astype(jnp.bfloat16)
    matrix = (
        dense_blocks.reshape(groups, groups, BASIS, BASIS)
        .transpose(0, 2, 1, 3)
        .reshape(groups * BASIS, groups * BASIS)
    )
    stacked = basis.reshape(groups * BASIS, EXT3)
    projected = jnp.dot(matrix, stacked, preferred_element_type=jnp.float32)
    box = (
        jnp.sum(stacked.astype(jnp.float32) * projected, axis=0)
        .reshape(EXT, 2, LANES)
        .transpose(1, 0, 2)
    )
    box = merged_z(box, "gz")
    y_low, y_high = merged(box[0], box[1], "gy")
    box = jnp.stack([y_low, y_high])
    x_low, x_high = merged(box[:, : EXT // 2], box[:, EXT // 2 :], "gx", forward=True)
    potential_ext = slater_potential(jnp.concatenate([x_low, x_high], axis=1))
    potential = potential_ext.reshape(2, EXT, EXT // 2, EXT)[:, RIM : RIM + CELLS, :, RIM : RIM + CELLS]
    potential = jnp.concatenate([potential[0, :, RIM:], potential[1, :, :RIM]], axis=1)
    potential_row = potential_ext.transpose(1, 0, 2).reshape(EXT3)
    weighted = (stacked.astype(jnp.float32) * potential_row[None, :]).astype(jnp.bfloat16)
    ks_full = (
        lax.dot_general(
            weighted, stacked, (((1,), (1,)), ((), ())), preferred_element_type=jnp.float32
        )
        * GRID_WEIGHT
    )
    ks_table = (
        ks_full.reshape(groups, BASIS, groups, BASIS)
        .transpose(0, 2, 1, 3)
        .reshape(groups * groups, square)
    )
    pair_blocks = jnp.take(ks_table, pair_codes, axis=0).astype(jnp.bfloat16)
    owners = lax.axis_size("gx") * lax.axis_size("gy")
    capacity = max(2, 2 * pairs // owners)
    owner_ids = owner[:, 0]
    order_ids = jnp.arange(pairs, dtype=jnp.int32)
    earlier = (owner_ids[:, None] == owner_ids[None, :]) & (order_ids[:, None] > order_ids[None, :])
    rank_within = jnp.sum(earlier.astype(jnp.int32), axis=1)
    positions = owner_ids * capacity + rank_within
    slot_match = jnp.arange(owners * capacity, dtype=jnp.int32)[:, None] == positions[None, :]
    send_blocks = jnp.dot(
        slot_match.astype(jnp.bfloat16), pair_blocks, preferred_element_type=jnp.float32
    ).astype(jnp.bfloat16)
    send_slots = jnp.sum(jnp.where(slot_match, owner_slot[None, :] + 1, 0), axis=1) - 1
    got_blocks, got_slots = (
        lax.all_to_all(
            send_blocks.reshape(owners, capacity * square // LANES, LANES),
            ("gx", "gy"),
            split_axis=0,
            concat_axis=0,
            tiled=True,
        ),
        lax.all_to_all(
            send_slots.reshape(owners, capacity),
            ("gx", "gy"),
            split_axis=0,
            concat_axis=0,
            tiled=True,
        ),
    )
    got_blocks = got_blocks.reshape(owners * capacity, square)
    got_slots = got_slots.reshape(owners * capacity)
    store_match = (jnp.arange(pairs, dtype=jnp.int32)[:, None] == got_slots[None, :]).astype(
        jnp.bfloat16
    )
    ks_blocks = jnp.dot(store_match, got_blocks, preferred_element_type=jnp.float32).astype(
        jnp.bfloat16
    )
    return (ks_blocks, potential)


def solution(mesh):
    return jax.shard_map(
        per_device,
        mesh=mesh,
        in_specs=(
            P(("gx", "gy", "gz"), None, None),
            P(("gx", "gy", "gz"), None),
            P(None, ("gx", "gy", "gz")),
            P(("gx", "gy", "gz"), None),
            P(("gx", "gy", "gz")),
        ),
        out_specs=(P(("gx", "gy", "gz"), None), P("gx", "gy", "gz")),
        check_vma=False,
    )
```

```python
import functools

import jax
import jax.numpy as jnp
from jax import lax
from jax.experimental import pallas as pl
from jax.experimental.pallas import tpu as pltpu
from jax.sharding import PartitionSpec as P

BASIS = 64
CELLS = 8
RIM = 4
EXT = 16
EXT3 = 4096
LANES = 128

XC_COEF = 0.9847450218426965
GRID_WEIGHT = 0.015625


def slater_potential(density):
    return -XC_COEF * density / jnp.cbrt(density * density + 1.0)


def neighbour_swaps(count, first):
    pairs = []
    for low in range(first, count + first, 2):
        left, right = low % count, (low + 1) % count
        pairs += [(left, right), (right, left)]
    return pairs


def merged(low, high, axis, forward=False):
    count = lax.axis_size(axis)
    if count == 2:
        got = lax.ppermute(jnp.stack([high, low]), axis, neighbour_swaps(count, 0))
        return low + got[0], high + got[1]
    odd = lax.axis_index(axis) % 2 == 1
    near, far = jnp.where(odd, low, high), jnp.where(odd, high, low)
    if forward and count == 4:
        got = lax.ppermute(jnp.stack([near, far]), axis, neighbour_swaps(count, 0))
        near = near + got[0]
        far = far + lax.ppermute(got[1], axis, [(i, i ^ 2) for i in range(count)])
    else:
        got = lax.ppermute(near, axis, neighbour_swaps(count, 0))
        other = lax.ppermute(far, axis, neighbour_swaps(count, 1))
        near, far = near + got, far + other
    return jnp.where(odd, near, far), jnp.where(odd, far, near)


def merged_z(box, swapped, axis):
    count = lax.axis_size(axis)
    if count == 2:
        return box + lax.ppermute(swapped, axis, neighbour_swaps(count, 0))
    odd = lax.axis_index(axis) % 2 == 1
    lane = lax.broadcasted_iota(jnp.int32, box.shape, box.ndim - 1)
    in_high = lane % EXT >= EXT // 2
    first = lax.ppermute(swapped, axis, neighbour_swaps(count, 0))
    second = lax.ppermute(swapped, axis, neighbour_swaps(count, 1))
    return box + jnp.where(in_high != odd, first, second)


def collocate_kernel(groups, pair_groups, blocks, basis, box, swapped, table, spread, matrix, arrived):
    rows = groups * BASIS
    chunk = 2 * EXT * EXT
    copies = []
    for c in range(EXT3 // chunk):
        cells = pl.ds(c * chunk, chunk)
        copies.append(
            pltpu.make_async_copy(basis.at[:, cells], table.at[:, cells], arrived.at[c])
        )
        copies[-1].start()
    pairs = blocks.shape[0]
    in_low = lax.broadcasted_iota(jnp.int32, (pairs, LANES), 1) < BASIS
    for j in range(BASIS // 2):
        two_rows = blocks[:, j * LANES : (j + 1) * LANES].astype(jnp.float32)
        turned = pltpu.roll(two_rows, BASIS, axis=1)
        spread[pl.ds(2 * j, pairs, stride=BASIS), :] = jnp.where(in_low, two_rows, turned)
        spread[pl.ds(2 * j + 1, pairs, stride=BASIS), :] = jnp.where(in_low, turned, two_rows)
    matrix[...] = jnp.zeros_like(matrix)
    half_of_lane = lax.broadcasted_iota(jnp.int32, (BASIS, LANES), 1) // BASIS

    def place(p, carry):
        first, second = pair_groups[0, p], pair_groups[1, p]
        at = (
            pl.ds(pl.multiple_of(first * BASIS, BASIS), BASIS),
            pl.ds(pl.multiple_of((second // 2) * LANES, LANES), LANES),
        )
        block = spread[pl.ds(pl.multiple_of(p * BASIS, BASIS), BASIS), :]
        matrix[at] = jnp.where(half_of_lane == second % 2, block, matrix[at])
        return carry

    lax.fori_loop(0, pairs, place, 0)
    dense = matrix[:, :rows].astype(jnp.bfloat16)
    for c in range(EXT3 // chunk):
        copies[c].wait()
        values = table[:, c * chunk : (c + 1) * chunk]
        projected = jnp.dot(dense, values, preferred_element_type=jnp.float32)
        summed = jnp.sum(values.astype(jnp.float32) * projected, axis=0, keepdims=True)
        for t in range(chunk // LANES):
            box[t % 2, 2 * c + t // 2, :] = summed[0, t * LANES : (t + 1) * LANES]
    lane = lax.broadcasted_iota(jnp.int32, (EXT, LANES), 1)
    for half in range(2):
        cells = box[half]
        swapped[half] = jnp.where(
            lane % EXT < EXT // 2,
            pltpu.roll(cells, LANES - EXT // 2, axis=1),
            pltpu.roll(cells, EXT // 2, axis=1),
        )


def collocated(basis, density_blocks, pair_groups):
    groups, pairs = basis.shape[0], density_blocks.shape[0]
    rows = groups * BASIS
    vmem, smem = pl.BlockSpec(memory_space=pltpu.VMEM), pl.BlockSpec(memory_space=pltpu.SMEM)
    return pl.pallas_call(
        functools.partial(collocate_kernel, groups),
        name="collocate",
        out_shape=(
            jax.ShapeDtypeStruct((2, EXT, LANES), jnp.float32),
            jax.ShapeDtypeStruct((2, EXT, LANES), jnp.float32),
            jax.ShapeDtypeStruct((rows, EXT3), basis.dtype),
        ),
        in_specs=[smem, vmem, pl.BlockSpec(memory_space=pl.ANY)],
        out_specs=[vmem, vmem, vmem],
        scratch_shapes=[
            pltpu.VMEM((pairs * BASIS, LANES), jnp.float32),
            pltpu.VMEM((rows, -(-rows // LANES) * LANES), jnp.float32),
            pltpu.SemaphoreType.DMA((EXT // 2,)),
        ],
        compiler_params=pltpu.CompilerParams(vmem_limit_bytes=24 << 20),
        cost_estimate=pl.CostEstimate(
            flops=2 * rows * rows * EXT3, bytes_accessed=2 * rows * EXT3, transcendentals=0
        ),
    )(pair_groups, density_blocks, basis.reshape(rows, EXT3))


def integrate_kernel(groups, capacity, pair_groups, places, potential, slots, table, send, total):
    rows = groups * BASIS
    pairs = places.shape[1]
    lines = BASIS // 2
    chunk = 4 * EXT * EXT
    for c in range(EXT3 // chunk):
        values = table[:, c * chunk : (c + 1) * chunk]
        weight = jnp.concatenate(
            [
                potential[t % 2, chunk // (2 * LANES) * c + t // 2 : chunk // (2 * LANES) * c + t // 2 + 1, :]
                for t in range(chunk // LANES)
            ],
            axis=1,
        )
        weighted = (values.astype(jnp.float32) * weight).astype(jnp.bfloat16)
        part = lax.dot_general(
            weighted, values, (((1,), (1,)), ((), ())), preferred_element_type=jnp.float32
        )
        if c == 0:
            total[:, :rows] = part
        else:
            total[:, :rows] += part
    send[:, capacity * lines :, :] = slots[...]
    in_low = lax.broadcasted_iota(jnp.int32, (lines, LANES), 1) < BASIS

    def place(p, carry):
        first, second = pair_groups[0, p], pair_groups[1, p]
        block = total[
            pl.ds(pl.multiple_of(first * BASIS, BASIS), BASIS),
            pl.ds(pl.multiple_of((second // 2) * LANES, LANES), LANES),
        ]
        turned = pltpu.roll(block, BASIS, axis=1)
        is_low = second % 2 == 0
        upper = jnp.where(is_low, block[:lines], turned[:lines])
        lower = jnp.where(is_low, turned[lines:], block[lines:])
        line = pl.multiple_of(places[1, p] * lines, lines)
        send[places[0, p], pl.ds(line, lines), :] = (
            jnp.where(in_low, upper, lower) * GRID_WEIGHT
        ).astype(send.dtype)
        return carry

    lax.fori_loop(0, pairs, place, 0)


def integrated(table, potential, slots, pair_groups, places, owners, capacity):
    rows = table.shape[0]
    vmem, smem = pl.BlockSpec(memory_space=pltpu.VMEM), pl.BlockSpec(memory_space=pltpu.SMEM)
    return pl.pallas_call(
        functools.partial(integrate_kernel, rows // BASIS, capacity),
        name="integrate",
        out_shape=jax.ShapeDtypeStruct(
            (owners, capacity * BASIS // 2 + slots.shape[1], LANES), jnp.bfloat16
        ),
        in_specs=[smem, smem, vmem, vmem, vmem],
        out_specs=vmem,
        scratch_shapes=[pltpu.VMEM((rows, -(-rows // LANES) * LANES), jnp.float32)],
        compiler_params=pltpu.CompilerParams(vmem_limit_bytes=24 << 20),
        cost_estimate=pl.CostEstimate(
            flops=2 * rows * rows * EXT3, bytes_accessed=2 * rows * EXT3, transcendentals=0
        ),
    )(pair_groups, places, potential, slots, table)


def store_kernel(capacity, got, store, total, slots_vector, slots, moved):
    lines = BASIS // 2
    sources = got.shape[0]
    stored = store.shape[0]
    for s in range(sources):
        slots_vector[s : s + 1, :] = (
            got[s, capacity * lines : capacity * lines + 8, :].astype(jnp.float32)[:1].astype(jnp.int32)
        )
    copy = pltpu.make_async_copy(slots_vector, slots, moved)
    copy.start()
    total[...] = jnp.zeros_like(total)
    copy.wait()

    def add(s, carry):
        for r in range(capacity):
            at = pl.ds(pl.multiple_of(slots[s, r] * lines, lines), lines)
            total[at, :] += got[s, r * lines : (r + 1) * lines, :].astype(jnp.float32)
        return carry

    lax.fori_loop(0, sources, add, 0)
    in_low = lax.broadcasted_iota(jnp.int32, (stored, LANES), 1) < BASIS
    for i in range(lines // 2):
        even = total[pl.ds(2 * i, stored, stride=lines), :]
        odd = total[pl.ds(2 * i + 1, stored, stride=lines), :]
        for j, row in (
            (i, jnp.where(in_low, even, pltpu.roll(odd, BASIS, axis=1))),
            (i + lines // 2, jnp.where(in_low, pltpu.roll(even, BASIS, axis=1), odd)),
        ):
            store[:, j * LANES : (j + 1) * LANES] = row.astype(store.dtype)


def stored_blocks(got, rows, capacity):
    vmem = pl.BlockSpec(memory_space=pltpu.VMEM)
    return pl.pallas_call(
        functools.partial(store_kernel, capacity),
        name="store",
        out_shape=jax.ShapeDtypeStruct((rows, BASIS * BASIS), jnp.bfloat16),
        in_specs=[vmem],
        out_specs=vmem,
        scratch_shapes=[
            pltpu.VMEM(((rows + 1) * BASIS // 2, LANES), jnp.float32),
            pltpu.VMEM((got.shape[0], LANES), jnp.int32),
            pltpu.SMEM((got.shape[0], LANES), jnp.int32),
            pltpu.SemaphoreType.DMA(()),
        ],
        compiler_params=pltpu.CompilerParams(vmem_limit_bytes=24 << 20),
        cost_estimate=pl.CostEstimate(
            flops=got.size, bytes_accessed=2 * got.size, transcendentals=0
        ),
    )(got)


def per_device(basis, density_blocks, pair_groups, owner, owner_slot):
    pairs = density_blocks.shape[0]
    owners = lax.axis_size("gx") * lax.axis_size("gy")
    capacity = max(2, 2 * pairs // owners)
    box, swapped, table = collocated(basis, density_blocks, pair_groups)

    owner_ids = owner[:, 0]
    order_ids = jnp.arange(pairs, dtype=jnp.int32)
    earlier = (owner_ids[:, None] == owner_ids[None, :]) & (order_ids[:, None] > order_ids[None, :])
    rank_within = jnp.sum(earlier.astype(jnp.int32), axis=1)
    places = jnp.stack([owner_ids, rank_within])
    lane_ids = jnp.arange(LANES, dtype=jnp.int32)
    chosen = (jnp.arange(owners, dtype=jnp.int32)[:, None, None] == owner_ids[None, None, :]) & (
        lane_ids[None, :, None] == rank_within[None, None, :]
    )
    slots = jnp.sum(jnp.where(chosen, owner_slot[None, None, :] - pairs, 0), axis=2) + pairs
    slots = jnp.broadcast_to(slots.astype(jnp.bfloat16)[:, None, :], (owners, 8, LANES))

    box = merged_z(box, swapped, "gz")
    y_low, y_high = merged(box[0], box[1], "gy")
    box = jnp.stack([y_low, y_high])
    x_low, x_high = merged(box[:, : EXT // 2], box[:, EXT // 2 :], "gx", forward=True)
    potential_ext = slater_potential(jnp.concatenate([x_low, x_high], axis=1))
    potential = potential_ext.reshape(2, EXT, EXT // 2, EXT)[:, RIM : RIM + CELLS, :, RIM : RIM + CELLS]
    potential = jnp.concatenate([potential[0, :, RIM:], potential[1, :, :RIM]], axis=1)

    send = integrated(table, potential_ext, slots, pair_groups, places, owners, capacity)
    got = lax.all_to_all(send, ("gx", "gy"), split_axis=0, concat_axis=0, tiled=True)
    return stored_blocks(got, pairs, capacity), potential


def solution(mesh):
    return jax.shard_map(
        per_device,
        mesh=mesh,
        in_specs=(
            P(("gx", "gy", "gz"), None, None),
            P(("gx", "gy", "gz"), None),
            P(None, ("gx", "gy", "gz")),
            P(("gx", "gy", "gz"), None),
            P(("gx", "gy", "gz")),
        ),
        out_specs=(P(("gx", "gy", "gz"), None), P("gx", "gy", "gz")),
        check_vma=False,
    )
```

```python
import functools

import jax
import jax.numpy as jnp
from jax import lax
from jax.experimental import pallas as pl
from jax.experimental.pallas import tpu as pltpu
from jax.sharding import PartitionSpec as P

BASIS = 64
CELLS = 8
RIM = 4
EXT = 16
EXT3 = 4096
LANES = 128

XC_COEF = 0.9847450218426965
GRID_WEIGHT = 0.015625


def slater_potential(density):
    return -XC_COEF * density / jnp.cbrt(density * density + 1.0)


def neighbour_swaps(count, first):
    pairs = []
    for low in range(first, count + first, 2):
        left, right = low % count, (low + 1) % count
        pairs += [(left, right), (right, left)]
    return pairs


def merged(low, high, axis, forward=False):
    count = lax.axis_size(axis)
    if count == 2:
        got = lax.ppermute(jnp.stack([high, low]), axis, neighbour_swaps(count, 0))
        return low + got[0], high + got[1]
    odd = lax.axis_index(axis) % 2 == 1
    near, far = jnp.where(odd, low, high), jnp.where(odd, high, low)
    if forward and count == 4:
        got = lax.ppermute(jnp.stack([near, far]), axis, neighbour_swaps(count, 0))
        near = near + got[0]
        far = far + lax.ppermute(got[1], axis, [(i, i ^ 2) for i in range(count)])
    else:
        got = lax.ppermute(near, axis, neighbour_swaps(count, 0))
        other = lax.ppermute(far, axis, neighbour_swaps(count, 1))
        near, far = near + got, far + other
    return jnp.where(odd, near, far), jnp.where(odd, far, near)


def merged_z(box, swapped, axis):
    count = lax.axis_size(axis)
    if count == 2:
        return box + lax.ppermute(swapped, axis, neighbour_swaps(count, 0))
    odd = lax.axis_index(axis) % 2 == 1
    lane = lax.broadcasted_iota(jnp.int32, box.shape, box.ndim - 1)
    in_high = lane % EXT >= EXT // 2
    first = lax.ppermute(swapped, axis, neighbour_swaps(count, 0))
    second = lax.ppermute(swapped, axis, neighbour_swaps(count, 1))
    return box + jnp.where(in_high != odd, first, second)


def resident_cells():
    return 8 * EXT * EXT


def fetches(basis, head, tail, arrived, chunk, first):
    kept = head.shape[1]
    copies = []
    for c in range(first, EXT3 // chunk):
        source = basis.at[:, pl.ds(c * chunk, chunk)]
        begin = c * chunk if c * chunk < kept else c * chunk - kept
        place = (head if c * chunk < kept else tail).at[:, pl.ds(begin, chunk)]
        copies.append((pltpu.make_async_copy(source, place, arrived.at[c]), place))
    return copies


def collocate_kernel(
    groups, pair_groups, blocks, basis, box, swapped, head,
    tail, codes, local, spread, matrix, owner_of, arrived, staged,
):
    pairs = blocks.shape[0]
    pitch = BASIS + 1
    codes_copy = pltpu.make_async_copy(pair_groups, codes, staged.at[0])
    blocks_copy = pltpu.make_async_copy(blocks, local, staged.at[1])
    codes_copy.start()
    blocks_copy.start()
    copies = fetches(basis, head, tail, arrived, 2 * EXT * EXT, 0)
    for copy, _ in copies:
        copy.start()
    spread[pl.ds(pairs * pitch, BASIS), :] = jnp.zeros((BASIS, LANES), jnp.float32)
    codes_copy.wait()
    for code in range(groups * groups):
        owner_of[code] = pairs
    for p in range(pairs):
        owner_of[codes[0, p] * groups + codes[1, p]] = p
    blocks_copy.wait()
    in_low = lax.broadcasted_iota(jnp.int32, (pairs, LANES), 1) < BASIS
    for j in range(BASIS // 2):
        two_rows = local[:, j * LANES : (j + 1) * LANES].astype(jnp.float32)
        turned = pltpu.roll(two_rows, BASIS, axis=1)
        spread[pl.ds(2 * j, pairs, stride=pitch), :] = jnp.where(in_low, two_rows, turned)
        spread[pl.ds(2 * j + 1, pairs, stride=pitch), :] = jnp.where(in_low, turned, two_rows)
    left = lax.broadcasted_iota(jnp.int32, (BASIS, LANES), 1) < BASIS
    for first in range(groups):
        for second in range(0, groups, 2):
            code = first * groups + second
            block = spread[pl.ds(owner_of[code] * pitch, BASIS), :]
            if second + 1 < groups:
                block = jnp.where(left, block, spread[pl.ds(owner_of[code + 1] * pitch, BASIS), :])
            matrix[
                first * BASIS : (first + 1) * BASIS, second * BASIS : second * BASIS + LANES
            ] = block.astype(matrix.dtype)
    dense = matrix[:, : groups * BASIS]
    for c, (copy, place) in enumerate(copies):
        copy.wait()
        values = place[...]
        projected = jnp.dot(dense, values, preferred_element_type=jnp.float32)
        summed = jnp.sum(values.astype(jnp.float32) * projected, axis=0, keepdims=True)
        for t in range(summed.shape[1] // LANES):
            box[t % 2, 2 * c + t // 2, :] = summed[0, t * LANES : (t + 1) * LANES]
    lane = lax.broadcasted_iota(jnp.int32, (EXT, LANES), 1)
    for half in range(2):
        cells = box[half]
        swapped[half] = jnp.where(
            lane % EXT < EXT // 2,
            pltpu.roll(cells, LANES - EXT // 2, axis=1),
            pltpu.roll(cells, EXT // 2, axis=1),
        )


def collocated(basis, density_blocks, pair_groups):
    rows, pairs = basis.shape[0], density_blocks.shape[0]
    groups = rows // BASIS
    kept = resident_cells()
    vmem, hbm = pl.BlockSpec(memory_space=pltpu.VMEM), pl.BlockSpec(memory_space=pltpu.HBM)
    return pl.pallas_call(
        functools.partial(collocate_kernel, groups),
        name="collocate",
        out_shape=(
            jax.ShapeDtypeStruct((2, EXT, LANES), jnp.float32),
            jax.ShapeDtypeStruct((2, EXT, LANES), jnp.float32),
            jax.ShapeDtypeStruct((rows, kept), basis.dtype),
        ),
        in_specs=[hbm, hbm, hbm],
        out_specs=[vmem, vmem, vmem],
        scratch_shapes=[
            pltpu.VMEM((rows, EXT3 - kept), basis.dtype),
            pltpu.SMEM(pair_groups.shape, jnp.int32),
            pltpu.VMEM(density_blocks.shape, density_blocks.dtype),
            pltpu.VMEM(((pairs + 1) * (BASIS + 1) + 7, LANES), jnp.float32),
            pltpu.VMEM((rows, -(-rows // LANES) * LANES), jnp.bfloat16),
            pltpu.SMEM((groups * groups,), jnp.int32),
            pltpu.SemaphoreType.DMA((EXT // 2,)),
            pltpu.SemaphoreType.DMA((2,)),
        ],
        compiler_params=pltpu.CompilerParams(vmem_limit_bytes=24 << 20),
        cost_estimate=pl.CostEstimate(
            flops=2 * rows * rows * EXT3, bytes_accessed=2 * rows * EXT3, transcendentals=0
        ),
    )(*[pltpu.with_memory_space_constraint(x, pltpu.HBM) for x in (pair_groups, density_blocks, basis)])


def integrate_kernel(
    groups, capacity, lines_of, potential, slots, head, basis, send, tail, total, arrived
):
    rows = groups * BASIS
    lines = BASIS // 2
    planes = 4
    chunk = planes * EXT * EXT
    kept = head.shape[1]
    copies = fetches(basis, head, tail, arrived, chunk, kept // chunk)
    for copy, _ in copies:
        copy.start()
    send[:, capacity * lines : capacity * lines + slots.shape[1], :] = slots[...]
    for c in range(EXT3 // chunk):
        if c * chunk < kept:
            values = head[:, c * chunk : (c + 1) * chunk]
        else:
            copy, place = copies[c - kept // chunk]
            copy.wait()
            values = place[...]
        weight = jnp.concatenate(
            [
                potential[t % 2, planes * c + t // 2 : planes * c + t // 2 + 1, :]
                for t in range(chunk // LANES)
            ],
            axis=1,
        )
        weighted = (values.astype(jnp.float32) * weight).astype(jnp.bfloat16)
        part = lax.dot_general(
            weighted, values, (((1,), (1,)), ((), ())), preferred_element_type=jnp.float32
        )
        if c == 0:
            total[:, :rows] = part
        else:
            total[:, :rows] += part
    left = lax.broadcasted_iota(jnp.int32, (lines, LANES), 1) < BASIS
    for first in range(groups):
        for second in range(groups):
            code = first * groups + second
            begin = second // 2 * LANES
            upper = total[first * BASIS : first * BASIS + lines, begin : begin + LANES]
            lower = total[first * BASIS + lines : (first + 1) * BASIS, begin : begin + LANES]
            if second % 2 == 0:
                lower = pltpu.roll(lower, BASIS, axis=1)
            else:
                upper = pltpu.roll(upper, BASIS, axis=1)
            line = pl.multiple_of(lines_of[1, code], lines)
            send[lines_of[0, code], pl.ds(line, lines), :] = (
                jnp.where(left, upper, lower) * GRID_WEIGHT
            ).astype(send.dtype)


def integrated(head, basis, potential, slots, lines_of, owners, capacity):
    rows = basis.shape[0]
    kept = head.shape[1]
    vmem, hbm = pl.BlockSpec(memory_space=pltpu.VMEM), pl.BlockSpec(memory_space=pltpu.HBM)
    return pl.pallas_call(
        functools.partial(integrate_kernel, rows // BASIS, capacity),
        name="integrate",
        out_shape=jax.ShapeDtypeStruct(
            (owners, capacity * BASIS // 2 + slots.shape[1], LANES), jnp.bfloat16
        ),
        in_specs=[pl.BlockSpec(memory_space=pltpu.SMEM), vmem, vmem, vmem, hbm],
        out_specs=vmem,
        scratch_shapes=[
            pltpu.VMEM((rows, EXT3 - kept), basis.dtype),
            pltpu.VMEM((rows, -(-rows // LANES) * LANES), jnp.float32),
            pltpu.SemaphoreType.DMA((EXT // 2,)),
        ],
        compiler_params=pltpu.CompilerParams(vmem_limit_bytes=24 << 20),
        cost_estimate=pl.CostEstimate(
            flops=2 * rows * rows * EXT3, bytes_accessed=2 * rows * EXT3, transcendentals=0
        ),
    )(lines_of, potential, slots, head, pltpu.with_memory_space_constraint(basis, pltpu.HBM))


def store_kernel(capacity, got, store, total, slots_vector, slots, moved):
    lines = BASIS // 2
    pitch = lines + 1
    sources = got.shape[0]
    stored = store.shape[0]
    for s in range(sources):
        slots_vector[s : s + 1, :] = (
            got[s, capacity * lines : capacity * lines + 8, :].astype(jnp.float32)[:1].astype(jnp.int32)
        )
    copy = pltpu.make_async_copy(slots_vector, slots, moved)
    copy.start()
    total[...] = jnp.zeros_like(total)
    copy.wait()

    def add(s, carry):
        for r in range(capacity):
            at = pl.ds(slots[s, r] * pitch, lines)
            total[at, :] += got[s, r * lines : (r + 1) * lines, :].astype(jnp.float32)
        return carry

    lax.fori_loop(0, sources, add, 0)
    in_low = lax.broadcasted_iota(jnp.int32, (stored, LANES), 1) < BASIS
    for i in range(lines // 2):
        even = total[pl.ds(2 * i, stored, stride=pitch), :]
        odd = total[pl.ds(2 * i + 1, stored, stride=pitch), :]
        for j, row in (
            (i, jnp.where(in_low, even, pltpu.roll(odd, BASIS, axis=1))),
            (i + lines // 2, jnp.where(in_low, pltpu.roll(even, BASIS, axis=1), odd)),
        ):
            store[:, j * LANES : (j + 1) * LANES] = row.astype(store.dtype)


def stored_blocks(got, rows, capacity):
    vmem = pl.BlockSpec(memory_space=pltpu.VMEM)
    return pl.pallas_call(
        functools.partial(store_kernel, capacity),
        name="store",
        out_shape=jax.ShapeDtypeStruct((rows, BASIS * BASIS), jnp.bfloat16),
        in_specs=[vmem],
        out_specs=vmem,
        scratch_shapes=[
            pltpu.VMEM(((rows + 1) * (BASIS // 2 + 1) + 7, LANES), jnp.float32),
            pltpu.VMEM((got.shape[0], LANES), jnp.int32),
            pltpu.SMEM((got.shape[0], LANES), jnp.int32),
            pltpu.SemaphoreType.DMA(()),
        ],
        compiler_params=pltpu.CompilerParams(vmem_limit_bytes=24 << 20),
        cost_estimate=pl.CostEstimate(
            flops=got.size, bytes_accessed=2 * got.size, transcendentals=0
        ),
    )(got)


def per_device(basis, density_blocks, pair_groups, owner, owner_slot):
    pairs = density_blocks.shape[0]
    owners = lax.axis_size("gx") * lax.axis_size("gy")
    capacity = max(2, 2 * pairs // owners)
    groups = basis.shape[0]
    basis = basis.reshape(groups * BASIS, EXT3)
    box, swapped, head = collocated(basis, density_blocks, pair_groups)

    owner_ids = owner[:, 0]
    order_ids = jnp.arange(pairs, dtype=jnp.int32)
    earlier = (owner_ids[:, None] == owner_ids[None, :]) & (order_ids[:, None] > order_ids[None, :])
    rank_within = jnp.sum(earlier.astype(jnp.int32), axis=1)
    counts = jnp.sum((owner_ids[None, :] == jnp.arange(owners)[:, None]).astype(jnp.int32), axis=1)
    least = jnp.min(counts * owners + jnp.arange(owners))
    free = jnp.stack([least % owners, least // owners])
    pair_codes = pair_groups[0] * groups + pair_groups[1]
    present = jnp.arange(groups * groups, dtype=jnp.int32)[:, None] == pair_codes[None, :]
    places = jnp.stack([owner_ids, rank_within]) - free[:, None]
    places = jnp.sum(jnp.where(present[None], places[:, None, :], 0), axis=2) + free[:, None]
    lines_of = places * jnp.array([1, BASIS // 2], dtype=jnp.int32)[:, None]
    lane_ids = jnp.arange(LANES, dtype=jnp.int32)
    chosen = (jnp.arange(owners, dtype=jnp.int32)[:, None, None] == owner_ids[None, None, :]) & (
        lane_ids[None, :, None] == rank_within[None, None, :]
    )
    slots = jnp.sum(jnp.where(chosen, owner_slot[None, None, :] - pairs, 0), axis=2) + pairs
    slots = jnp.broadcast_to(slots.astype(jnp.bfloat16)[:, None, :], (owners, 8, LANES))

    box = merged_z(box, swapped, "gz")
    y_low, y_high = merged(box[0], box[1], "gy")
    box = jnp.stack([y_low, y_high])
    x_low, x_high = merged(box[:, : EXT // 2], box[:, EXT // 2 :], "gx", forward=True)
    potential_ext = slater_potential(jnp.concatenate([x_low, x_high], axis=1))
    potential = potential_ext.reshape(2, EXT, EXT // 2, EXT)[:, RIM : RIM + CELLS, :, RIM : RIM + CELLS]
    potential = jnp.concatenate([potential[0, :, RIM:], potential[1, :, :RIM]], axis=1)

    send = integrated(head, basis, potential_ext, slots, lines_of, owners, capacity)
    got = lax.all_to_all(send, ("gx", "gy"), split_axis=0, concat_axis=0, tiled=True)
    return stored_blocks(got, pairs, capacity), potential


def solution(mesh):
    return jax.shard_map(
        per_device,
        mesh=mesh,
        in_specs=(
            P(("gx", "gy", "gz"), None, None),
            P(("gx", "gy", "gz"), None),
            P(None, ("gx", "gy", "gz")),
            P(("gx", "gy", "gz"), None),
            P(("gx", "gy", "gz")),
        ),
        out_specs=(P(("gx", "gy", "gz"), None), P("gx", "gy", "gz")),
        check_vma=False,
    )
```

```python
import functools

import jax
import jax.numpy as jnp
from jax import lax
from jax.experimental import pallas as pl
from jax.experimental.pallas import tpu as pltpu
from jax.sharding import PartitionSpec as P

BASIS = 64
CELLS = 8
RIM = 4
EXT = 16
EXT3 = 4096
LANES = 128

XC_COEF = 0.9847450218426965
GRID_WEIGHT = 0.015625


def slater_potential(density):
    return -XC_COEF * density / jnp.cbrt(density * density + 1.0)


def neighbour_swaps(count, first):
    pairs = []
    for low in range(first, count + first, 2):
        left, right = low % count, (low + 1) % count
        pairs += [(left, right), (right, left)]
    return pairs


def merged(low, high, axis):
    count = lax.axis_size(axis)
    if count == 2:
        got = lax.ppermute(jnp.stack([high, low]), axis, neighbour_swaps(count, 0))
        return low + got[0], high + got[1]
    odd = lax.axis_index(axis) % 2 == 1
    near, far = jnp.where(odd, low, high), jnp.where(odd, high, low)
    near = near + lax.ppermute(near, axis, neighbour_swaps(count, 0))
    far = far + lax.ppermute(far, axis, neighbour_swaps(count, 1))
    return jnp.where(odd, near, far), jnp.where(odd, far, near)


def merged_z(box, swapped, axis):
    count = lax.axis_size(axis)
    if count == 2:
        return box + lax.ppermute(swapped, axis, neighbour_swaps(count, 0))
    odd = lax.axis_index(axis) % 2 == 1
    lane = lax.broadcasted_iota(jnp.int32, box.shape, box.ndim - 1)
    in_high = lane % EXT >= EXT // 2
    first = lax.ppermute(swapped, axis, neighbour_swaps(count, 0))
    second = lax.ppermute(swapped, axis, neighbour_swaps(count, 1))
    return box + jnp.where(in_high != odd, first, second)


def resident_cells():
    return 12 * EXT * EXT


def fetches(basis, head, tail, arrived, chunk, first):
    kept = head.shape[1]
    copies = []
    for c in range(first, EXT3 // chunk):
        source = basis.at[:, pl.ds(c * chunk, chunk)]
        begin = c * chunk if c * chunk < kept else c * chunk - kept
        place = (head if c * chunk < kept else tail).at[:, pl.ds(begin, chunk)]
        copies.append((pltpu.make_async_copy(source, place, arrived.at[c]), place))
    return copies


def collocate_kernel(
    groups, pair_groups, blocks, basis, box, swapped, head,
    tail, codes, local, spread, matrix, owner_of, arrived, staged,
):
    pairs = blocks.shape[0]
    pitch = BASIS + 1
    codes_copy = pltpu.make_async_copy(pair_groups, codes, staged.at[0])
    blocks_copy = pltpu.make_async_copy(blocks, local, staged.at[1])
    ahead, planes = 2, 4
    copies = fetches(basis, head, tail, arrived, planes * EXT * EXT, 0)
    for copy in [codes_copy, blocks_copy] + [copy for copy, _ in copies[:ahead]]:
        copy.start()
    spread[pl.ds(pairs * pitch, BASIS), :] = jnp.zeros((BASIS, LANES), jnp.float32)
    codes_copy.wait()
    for code in range(groups * groups):
        owner_of[code] = pairs
    for p in range(pairs):
        owner_of[codes[0, p] * groups + codes[1, p]] = p
    blocks_copy.wait()
    in_low = lax.broadcasted_iota(jnp.int32, (pairs, LANES), 1) < BASIS
    for j in range(BASIS // 2):
        two_rows = local[:, j * LANES : (j + 1) * LANES].astype(jnp.float32)
        turned = pltpu.roll(two_rows, BASIS, axis=1)
        spread[pl.ds(2 * j, pairs, stride=pitch), :] = jnp.where(in_low, two_rows, turned)
        spread[pl.ds(2 * j + 1, pairs, stride=pitch), :] = jnp.where(in_low, turned, two_rows)
    left = lax.broadcasted_iota(jnp.int32, (BASIS, LANES), 1) < BASIS
    for first in range(groups):
        for second in range(0, groups, 2):
            code = first * groups + second
            block = spread[pl.ds(owner_of[code] * pitch, BASIS), :]
            if second + 1 < groups:
                block = jnp.where(left, block, spread[pl.ds(owner_of[code + 1] * pitch, BASIS), :])
            matrix[
                first * BASIS : (first + 1) * BASIS, second * BASIS : second * BASIS + LANES
            ] = block.astype(matrix.dtype)
    dense = matrix[:, : groups * BASIS]
    for c, (copy, place) in enumerate(copies):
        copy.wait()
        if c + ahead < len(copies):
            copies[c + ahead][0].start()
        values = place[...]
        projected = jnp.dot(dense, values, preferred_element_type=jnp.float32)
        summed = jnp.sum(values.astype(jnp.float32) * projected, axis=0, keepdims=True)
        for t in range(summed.shape[1] // LANES):
            box[t % 2, planes * c + t // 2, :] = summed[0, t * LANES : (t + 1) * LANES]
    lane = lax.broadcasted_iota(jnp.int32, (EXT, LANES), 1)
    for half in range(2):
        cells = box[half]
        swapped[half] = jnp.where(
            lane % EXT < EXT // 2,
            pltpu.roll(cells, LANES - EXT // 2, axis=1),
            pltpu.roll(cells, EXT // 2, axis=1),
        )


def collocated(basis, density_blocks, pair_groups):
    rows, pairs = basis.shape[0], density_blocks.shape[0]
    groups = rows // BASIS
    kept = resident_cells()
    vmem, hbm = pl.BlockSpec(memory_space=pltpu.VMEM), pl.BlockSpec(memory_space=pltpu.HBM)
    return pl.pallas_call(
        functools.partial(collocate_kernel, groups),
        name="collocate",
        out_shape=(
            jax.ShapeDtypeStruct((2, EXT, LANES), jnp.float32),
            jax.ShapeDtypeStruct((2, EXT, LANES), jnp.float32),
            jax.ShapeDtypeStruct((rows, kept), basis.dtype),
        ),
        in_specs=[hbm, hbm, hbm],
        out_specs=[vmem, vmem, vmem],
        scratch_shapes=[
            pltpu.VMEM((rows, EXT3 - kept), basis.dtype),
            pltpu.SMEM(pair_groups.shape, jnp.int32),
            pltpu.VMEM(density_blocks.shape, density_blocks.dtype),
            pltpu.VMEM(((pairs + 1) * (BASIS + 1) + 7, LANES), jnp.float32),
            pltpu.VMEM((rows, -(-rows // LANES) * LANES), jnp.bfloat16),
            pltpu.SMEM((groups * groups,), jnp.int32),
            pltpu.SemaphoreType.DMA((EXT // 2,)),
            pltpu.SemaphoreType.DMA((2,)),
        ],
        compiler_params=pltpu.CompilerParams(vmem_limit_bytes=24 << 20),
        cost_estimate=pl.CostEstimate(
            flops=2 * rows * rows * EXT3, bytes_accessed=2 * rows * EXT3, transcendentals=0
        ),
    )(*in_hbm(pair_groups, density_blocks, basis))


def tabulate(groups, capacity, codes, owner, slot, counts, place, slot_rows):
    pairs, owners = codes.shape[1], counts.shape[0]
    for o in range(owners):
        counts[o] = 0
    for code in range(groups * groups):
        place[0, code] = -1
    slot_rows[...] = jnp.full(slot_rows.shape, pairs, jnp.float32)
    lane = lax.broadcasted_iota(jnp.int32, (1, LANES), 1)
    for p in range(pairs):
        o = owner[0, p]
        rank = counts[o]
        counts[o] = rank + 1
        code = codes[0, p] * groups + codes[1, p]
        place[0, code] = o
        place[1, code] = rank
        row = slot_rows[pl.ds(o, 1), :]
        slot_rows[pl.ds(o, 1), :] = jnp.where(lane == rank, slot[0, p].astype(jnp.float32), row)
    free_owner, free_rank = jnp.int32(0), counts[0]
    for o in range(1, owners):
        fewer = counts[o] < free_rank
        free_owner = jnp.where(fewer, o, free_owner)
        free_rank = jnp.where(fewer, counts[o], free_rank)
    for code in range(groups * groups):
        absent = place[0, code] < 0
        place[1, code] = jnp.where(absent, free_rank, place[1, code])
        place[0, code] = jnp.where(absent, free_owner, place[0, code])


def integrate_kernel(
    groups, capacity, pair_groups, owner, owner_slot, potential, head, basis, send,
    tail, total, slot_rows, codes, owners_of, slots_of, counts, place, arrived, staged,
):
    rows = groups * BASIS
    lines = BASIS // 2
    planes = 4
    chunk = planes * EXT * EXT
    kept = head.shape[1]
    tables = [
        pltpu.make_async_copy(source, target, staged.at[i])
        for i, (source, target) in enumerate(
            [(pair_groups, codes), (owner, owners_of), (owner_slot, slots_of)]
        )
    ]
    for copy in tables:
        copy.start()
    copies = fetches(basis, head, tail, arrived, chunk, kept // chunk)
    for copy, _ in copies:
        copy.start()
    for c in range(EXT3 // chunk):
        if c * chunk < kept:
            values = head[:, c * chunk : (c + 1) * chunk]
        else:
            copy, fetched = copies[c - kept // chunk]
            copy.wait()
            values = fetched[...]
        weight = jnp.concatenate(
            [
                potential[t % 2, planes * c + t // 2 : planes * c + t // 2 + 1, :]
                for t in range(chunk // LANES)
            ],
            axis=1,
        )
        weighted = (values.astype(jnp.float32) * weight).astype(jnp.bfloat16)
        part = lax.dot_general(
            weighted, values, (((1,), (1,)), ((), ())), preferred_element_type=jnp.float32
        )
        if c == 0:
            total[:, :rows] = part
            for copy in tables:
                copy.wait()
            tabulate(groups, capacity, codes, owners_of, slots_of, counts, place, slot_rows)
        else:
            total[:, :rows] += part
    for o in range(send.shape[0]):
        send[o, capacity * lines :, :] = jnp.broadcast_to(
            slot_rows[o : o + 1, :], (send.shape[1] - capacity * lines, LANES)
        ).astype(send.dtype)
    left = lax.broadcasted_iota(jnp.int32, (lines, LANES), 1) < BASIS
    for first in range(groups):
        for second in range(groups):
            code = first * groups + second
            begin = second // 2 * LANES
            upper = total[first * BASIS : first * BASIS + lines, begin : begin + LANES]
            lower = total[first * BASIS + lines : (first + 1) * BASIS, begin : begin + LANES]
            if second % 2 == 0:
                lower = pltpu.roll(lower, BASIS, axis=1)
            else:
                upper = pltpu.roll(upper, BASIS, axis=1)
            line = pl.multiple_of(place[1, code] * lines, lines)
            send[place[0, code], pl.ds(line, lines), :] = (
                jnp.where(left, upper, lower) * GRID_WEIGHT
            ).astype(send.dtype)


def in_hbm(*arrays):
    return [pltpu.with_memory_space_constraint(x, pltpu.HBM) for x in arrays]


def integrated(head, basis, potential, pair_groups, owner, owner_slot, owners, capacity):
    rows, pairs = basis.shape[0], pair_groups.shape[1]
    groups = rows // BASIS
    kept = head.shape[1]
    vmem, hbm = pl.BlockSpec(memory_space=pltpu.VMEM), pl.BlockSpec(memory_space=pltpu.HBM)
    return pl.pallas_call(
        functools.partial(integrate_kernel, groups, capacity),
        name="integrate",
        out_shape=jax.ShapeDtypeStruct((owners, capacity * BASIS // 2 + 8, LANES), jnp.bfloat16),
        in_specs=[hbm, hbm, hbm, vmem, vmem, hbm],
        out_specs=vmem,
        scratch_shapes=[
            pltpu.VMEM((rows, EXT3 - kept), basis.dtype),
            pltpu.VMEM((rows, -(-rows // LANES) * LANES), jnp.float32),
            pltpu.VMEM((owners, LANES), jnp.float32),
            pltpu.SMEM((2, pairs), jnp.int32),
            pltpu.SMEM((1, pairs), jnp.int32),
            pltpu.SMEM((1, pairs), jnp.int32),
            pltpu.SMEM((owners,), jnp.int32),
            pltpu.SMEM((2, groups * groups), jnp.int32),
            pltpu.SemaphoreType.DMA((EXT // 2,)),
            pltpu.SemaphoreType.DMA((3,)),
        ],
        compiler_params=pltpu.CompilerParams(vmem_limit_bytes=24 << 20),
        cost_estimate=pl.CostEstimate(
            flops=2 * rows * rows * EXT3, bytes_accessed=2 * rows * EXT3, transcendentals=0
        ),
    )(
        *in_hbm(pair_groups, owner.reshape(1, pairs), owner_slot.reshape(1, pairs)),
        potential,
        head,
        *in_hbm(basis),
    )


def store_kernel(capacity, got, store, total, slots_vector, slots, moved):
    lines = BASIS // 2
    pitch = lines + 1
    sources = got.shape[0]
    stored = store.shape[0]
    for s in range(sources):
        slots_vector[s : s + 1, :] = (
            got[s, capacity * lines : capacity * lines + 8, :].astype(jnp.float32)[:1].astype(jnp.int32)
        )
    copy = pltpu.make_async_copy(slots_vector, slots, moved)
    copy.start()
    total[...] = jnp.zeros_like(total)
    copy.wait()

    def add(s, carry):
        for r in range(capacity):
            at = pl.ds(slots[s, r] * pitch, lines)
            total[at, :] += got[s, r * lines : (r + 1) * lines, :].astype(jnp.float32)
        return carry

    lax.fori_loop(0, sources, add, 0)
    in_low = lax.broadcasted_iota(jnp.int32, (stored, LANES), 1) < BASIS
    for i in range(lines // 2):
        even = total[pl.ds(2 * i, stored, stride=pitch), :]
        odd = total[pl.ds(2 * i + 1, stored, stride=pitch), :]
        for j, row in (
            (i, jnp.where(in_low, even, pltpu.roll(odd, BASIS, axis=1))),
            (i + lines // 2, jnp.where(in_low, pltpu.roll(even, BASIS, axis=1), odd)),
        ):
            store[:, j * LANES : (j + 1) * LANES] = row.astype(store.dtype)


def stored_blocks(got, rows, capacity):
    vmem = pl.BlockSpec(memory_space=pltpu.VMEM)
    return pl.pallas_call(
        functools.partial(store_kernel, capacity),
        name="store",
        out_shape=jax.ShapeDtypeStruct((rows, BASIS * BASIS), jnp.bfloat16),
        in_specs=[vmem],
        out_specs=vmem,
        scratch_shapes=[
            pltpu.VMEM(((rows + 1) * (BASIS // 2 + 1) + 7, LANES), jnp.float32),
            pltpu.VMEM((got.shape[0], LANES), jnp.int32),
            pltpu.SMEM((got.shape[0], LANES), jnp.int32),
            pltpu.SemaphoreType.DMA(()),
        ],
        compiler_params=pltpu.CompilerParams(vmem_limit_bytes=24 << 20),
        cost_estimate=pl.CostEstimate(
            flops=got.size, bytes_accessed=2 * got.size, transcendentals=0
        ),
    )(got)


def per_device(basis, density_blocks, pair_groups, owner, owner_slot):
    pairs = density_blocks.shape[0]
    owners = lax.axis_size("gx") * lax.axis_size("gy")
    capacity = max(2, 2 * pairs // owners)
    groups = basis.shape[0]
    basis = basis.reshape(groups * BASIS, EXT3)
    box, swapped, head = collocated(basis, density_blocks, pair_groups)
    box = merged_z(box, swapped, "gz")
    y_low, y_high = merged(box[0], box[1], "gy")
    box = jnp.stack([y_low, y_high])
    x_low, x_high = merged(box[:, : EXT // 2], box[:, EXT // 2 :], "gx")
    potential_ext = slater_potential(jnp.concatenate([x_low, x_high], axis=1))
    potential = potential_ext.reshape(2, EXT, EXT // 2, EXT)[:, RIM : RIM + CELLS, :, RIM : RIM + CELLS]
    potential = jnp.concatenate([potential[0, :, RIM:], potential[1, :, :RIM]], axis=1)

    send = integrated(
        head, basis, potential_ext, pair_groups, owner, owner_slot, owners, capacity
    )
    got = lax.all_to_all(send, ("gx", "gy"), split_axis=0, concat_axis=0, tiled=True)
    return stored_blocks(got, pairs, capacity), potential


def solution(mesh):
    return jax.shard_map(
        per_device,
        mesh=mesh,
        in_specs=(
            P(("gx", "gy", "gz"), None, None),
            P(("gx", "gy", "gz"), None),
            P(None, ("gx", "gy", "gz")),
            P(("gx", "gy", "gz"), None),
            P(("gx", "gy", "gz")),
        ),
        out_specs=(P(("gx", "gy", "gz"), None), P("gx", "gy", "gz")),
        check_vma=False,
    )
```

```python
import functools

import jax
import jax.numpy as jnp
from jax import lax
from jax.experimental import pallas as pl
from jax.experimental.pallas import tpu as pltpu
from jax.sharding import PartitionSpec as P

BASIS = 64
CELLS = 8
RIM = 4
EXT = 16
EXT3 = 4096
LANES = 128

XC_COEF = 0.9847450218426965
GRID_WEIGHT = 0.015625


def slater_potential(density):
    return -XC_COEF * density / jnp.cbrt(density * density + 1.0)


def neighbour_swaps(count, first):
    pairs = []
    for low in range(first, count + first, 2):
        left, right = low % count, (low + 1) % count
        pairs += [(left, right), (right, left)]
    return pairs


def merged_halves(low, high, axis):
    count = lax.axis_size(axis)
    odd = lax.axis_index(axis) % 2 == 1
    near, far = jnp.where(odd, low, high), jnp.where(odd, high, low)
    near = near + lax.ppermute(near, axis, neighbour_swaps(count, 0))
    far = far + lax.ppermute(far, axis, neighbour_swaps(count, 1))
    return odd, near, far


def merged(low, high, axis):
    odd, near, far = merged_halves(low, high, axis)
    return jnp.where(odd, near, far), jnp.where(odd, far, near)


def merged_z(box, swapped, axis):
    count = lax.axis_size(axis)
    if count == 2:
        return box + lax.ppermute(swapped, axis, neighbour_swaps(count, 0))
    odd = lax.axis_index(axis) % 2 == 1
    lane = lax.broadcasted_iota(jnp.int32, box.shape, box.ndim - 1)
    in_high = lane % EXT >= EXT // 2
    first = lax.ppermute(swapped, axis, neighbour_swaps(count, 0))
    second = lax.ppermute(swapped, axis, neighbour_swaps(count, 1))
    return box + jnp.where(in_high != odd, first, second)


def halves():
    odd = lax.axis_index("gx") % 2
    return (1 - odd) * (EXT3 // 2), odd * (EXT3 // 2)


def collocate_kernel(
    groups, pair_groups, blocks, basis, box, swapped, near,
    far, codes, local, spread, matrix, owner_of, arrived, staged,
):
    pairs = blocks.shape[0]
    pitch = BASIS + 1
    codes_copy = pltpu.make_async_copy(pair_groups, codes, staged.at[0])
    blocks_copy = pltpu.make_async_copy(blocks, local, staged.at[1])
    ahead, planes = 2, 4
    cells = planes * EXT * EXT
    copies, plane_of = [], []
    for begin, half in zip(halves(), (near, far)):
        for c in range(half.shape[1] // cells):
            first = pl.multiple_of(begin + c * cells, LANES)
            place = half.at[:, pl.ds(c * cells, cells)]
            copies.append(
                (
                    pltpu.make_async_copy(
                        basis.at[:, pl.ds(first, cells)], place, arrived.at[len(copies)]
                    ),
                    place,
                )
            )
            plane_of.append(begin // (EXT * EXT) + c * planes)
    for copy in [codes_copy, blocks_copy] + [copy for copy, _ in copies[:ahead]]:
        copy.start()
    spread[pl.ds(pairs * pitch, BASIS), :] = jnp.zeros((BASIS, LANES), jnp.float32)
    codes_copy.wait()
    for code in range(groups * groups):
        owner_of[code] = pairs
    for p in range(pairs):
        owner_of[codes[0, p] * groups + codes[1, p]] = p
    blocks_copy.wait()
    in_low = lax.broadcasted_iota(jnp.int32, (pairs, LANES), 1) < BASIS
    for j in range(BASIS // 2):
        two_rows = local[:, j * LANES : (j + 1) * LANES].astype(jnp.float32)
        turned = pltpu.roll(two_rows, BASIS, axis=1)
        spread[pl.ds(2 * j, pairs, stride=pitch), :] = jnp.where(in_low, two_rows, turned)
        spread[pl.ds(2 * j + 1, pairs, stride=pitch), :] = jnp.where(in_low, turned, two_rows)
    left = lax.broadcasted_iota(jnp.int32, (BASIS, LANES), 1) < BASIS
    for first in range(groups):
        for second in range(0, groups, 2):
            code = first * groups + second
            block = spread[pl.ds(owner_of[code] * pitch, BASIS), :]
            if second + 1 < groups:
                block = jnp.where(left, block, spread[pl.ds(owner_of[code + 1] * pitch, BASIS), :])
            matrix[
                first * BASIS : (first + 1) * BASIS, second * BASIS : second * BASIS + LANES
            ] = block.astype(matrix.dtype)
    dense = matrix[:, : groups * BASIS]
    for c, (copy, place) in enumerate(copies):
        copy.wait()
        if c + ahead < len(copies):
            copies[c + ahead][0].start()
        values = place[...]
        projected = jnp.dot(dense, values, preferred_element_type=jnp.float32)
        summed = jnp.sum(values.astype(jnp.float32) * projected, axis=0, keepdims=True)
        for t in range(summed.shape[1] // LANES):
            box[t % 2, pl.ds(plane_of[c] + t // 2, 1), :] = summed[:, t * LANES : (t + 1) * LANES]
    lane = lax.broadcasted_iota(jnp.int32, (EXT, LANES), 1)
    for half in range(2):
        cells = box[half]
        swapped[half] = jnp.where(
            lane % EXT < EXT // 2,
            pltpu.roll(cells, LANES - EXT // 2, axis=1),
            pltpu.roll(cells, EXT // 2, axis=1),
        )


def collocated(basis, density_blocks, pair_groups):
    rows, pairs = basis.shape[0], density_blocks.shape[0]
    groups = rows // BASIS
    vmem, hbm = pl.BlockSpec(memory_space=pltpu.VMEM), pl.BlockSpec(memory_space=pltpu.HBM)
    return pl.pallas_call(
        functools.partial(collocate_kernel, groups),
        name="collocate",
        out_shape=(
            jax.ShapeDtypeStruct((2, EXT, LANES), jnp.float32),
            jax.ShapeDtypeStruct((2, EXT, LANES), jnp.float32),
            jax.ShapeDtypeStruct((rows, EXT3 // 2), basis.dtype),
        ),
        in_specs=[hbm, hbm, hbm],
        out_specs=[vmem, vmem, vmem],
        scratch_shapes=[
            pltpu.VMEM((rows, EXT3 // 2), basis.dtype),
            pltpu.SMEM(pair_groups.shape, jnp.int32),
            pltpu.VMEM(density_blocks.shape, density_blocks.dtype),
            pltpu.VMEM(((pairs + 1) * (BASIS + 1) + 7, LANES), jnp.float32),
            pltpu.VMEM((rows, padded(rows)), jnp.bfloat16),
            pltpu.SMEM((groups * groups,), jnp.int32),
            pltpu.SemaphoreType.DMA((EXT // 2,)),
            pltpu.SemaphoreType.DMA((2,)),
        ],
        compiler_params=pltpu.CompilerParams(vmem_limit_bytes=24 << 20),
        cost_estimate=pl.CostEstimate(
            flops=2 * rows * rows * EXT3, bytes_accessed=2 * rows * EXT3, transcendentals=0
        ),
    )(*in_hbm(pair_groups, density_blocks, basis))


def tabulate(groups, capacity, codes, owner, slot, counts, place, slot_rows):
    pairs, owners = codes.shape[1], counts.shape[0]
    for o in range(owners):
        counts[o] = 0
    for code in range(groups * groups):
        place[0, code] = -1
    slot_rows[...] = jnp.full(slot_rows.shape, pairs, jnp.float32)
    lane = lax.broadcasted_iota(jnp.int32, (1, LANES), 1)
    for p in range(pairs):
        o = owner[0, p]
        rank = counts[o]
        counts[o] = rank + 1
        code = codes[0, p] * groups + codes[1, p]
        place[0, code] = o
        place[1, code] = rank
        row = slot_rows[pl.ds(o, 1), :]
        slot_rows[pl.ds(o, 1), :] = jnp.where(lane == rank, slot[0, p].astype(jnp.float32), row)
    free_owner, free_rank = jnp.int32(0), counts[0]
    for o in range(1, owners):
        fewer = counts[o] < free_rank
        free_owner = jnp.where(fewer, o, free_owner)
        free_rank = jnp.where(fewer, counts[o], free_rank)
    for code in range(groups * groups):
        absent = place[0, code] < 0
        place[1, code] = jnp.where(absent, free_rank, place[1, code])
        place[0, code] = jnp.where(absent, free_owner, place[0, code])


def overlaps(table, potential, planes=4):
    cells = planes * EXT * EXT
    for c in range(table.shape[1] // cells):
        values = table[:, c * cells : (c + 1) * cells]
        weight = jnp.concatenate(
            [
                potential[t % 2, planes * c + t // 2 : planes * c + t // 2 + 1, :]
                for t in range(cells // LANES)
            ],
            axis=1,
        )
        weighted = (values.astype(jnp.float32) * weight).astype(jnp.bfloat16)
        yield lax.dot_general(
            weighted, values, (((1,), (1,)), ((), ())), preferred_element_type=jnp.float32
        )


def near_kernel(potential, near, basis, total, far, arrived):
    rows = near.shape[0]
    begin = pl.multiple_of(halves()[1], LANES)
    copy = pltpu.make_async_copy(basis.at[:, pl.ds(begin, far.shape[1])], far, arrived)
    copy.start()
    for c, part in enumerate(overlaps(near, potential)):
        if c == 0:
            total[:, :rows] = part
        else:
            total[:, :rows] += part
    copy.wait()


def far_kernel(
    groups, capacity, pair_groups, owner, owner_slot, potential, far, near_total, send,
    total, slot_rows, codes, owners_of, slots_of, counts, place, staged,
):
    rows = groups * BASIS
    lines = BASIS // 2
    tables = [
        pltpu.make_async_copy(source, target, staged.at[i])
        for i, (source, target) in enumerate(
            [(pair_groups, codes), (owner, owners_of), (owner_slot, slots_of)]
        )
    ]
    for copy in tables:
        copy.start()
    for c, part in enumerate(overlaps(far, potential)):
        if c == 0:
            total[:, :rows] = near_total[:, :rows] + part
            for copy in tables:
                copy.wait()
            tabulate(groups, capacity, codes, owners_of, slots_of, counts, place, slot_rows)
        else:
            total[:, :rows] += part
    for o in range(send.shape[0]):
        send[o, capacity * lines :, :] = jnp.broadcast_to(
            slot_rows[o : o + 1, :], (send.shape[1] - capacity * lines, LANES)
        ).astype(send.dtype)
    left = lax.broadcasted_iota(jnp.int32, (lines, LANES), 1) < BASIS
    for first in range(groups):
        for second in range(groups):
            code = first * groups + second
            begin = second // 2 * LANES
            upper = total[first * BASIS : first * BASIS + lines, begin : begin + LANES]
            lower = total[first * BASIS + lines : (first + 1) * BASIS, begin : begin + LANES]
            if second % 2 == 0:
                lower = pltpu.roll(lower, BASIS, axis=1)
            else:
                upper = pltpu.roll(upper, BASIS, axis=1)
            line = pl.multiple_of(place[1, code] * lines, lines)
            send[place[0, code], pl.ds(line, lines), :] = (
                jnp.where(left, upper, lower) * GRID_WEIGHT
            ).astype(send.dtype)


def in_hbm(*arrays):
    return [pltpu.with_memory_space_constraint(x, pltpu.HBM) for x in arrays]


def padded(rows):
    return -(-rows // LANES) * LANES


def integrated_near(near, basis, potential):
    rows = basis.shape[0]
    vmem, hbm = pl.BlockSpec(memory_space=pltpu.VMEM), pl.BlockSpec(memory_space=pltpu.HBM)
    return pl.pallas_call(
        near_kernel,
        name="integrate_near",
        out_shape=(
            jax.ShapeDtypeStruct((rows, padded(rows)), jnp.float32),
            jax.ShapeDtypeStruct((rows, EXT3 // 2), basis.dtype),
        ),
        in_specs=[vmem, vmem, hbm],
        out_specs=[vmem, vmem],
        scratch_shapes=[pltpu.SemaphoreType.DMA(())],
        compiler_params=pltpu.CompilerParams(vmem_limit_bytes=24 << 20),
        cost_estimate=pl.CostEstimate(
            flops=rows * rows * EXT3, bytes_accessed=2 * rows * EXT3, transcendentals=0
        ),
    )(potential, near, *in_hbm(basis))


def integrated_far(far, near_total, potential, pair_groups, owner, owner_slot, owners, capacity):
    rows, pairs = far.shape[0], pair_groups.shape[1]
    groups = rows // BASIS
    vmem, hbm = pl.BlockSpec(memory_space=pltpu.VMEM), pl.BlockSpec(memory_space=pltpu.HBM)
    return pl.pallas_call(
        functools.partial(far_kernel, groups, capacity),
        name="integrate_far",
        out_shape=jax.ShapeDtypeStruct((owners, capacity * BASIS // 2 + 8, LANES), jnp.bfloat16),
        in_specs=[hbm, hbm, hbm, vmem, vmem, vmem],
        out_specs=vmem,
        scratch_shapes=[
            pltpu.VMEM((rows, padded(rows)), jnp.float32),
            pltpu.VMEM((owners, LANES), jnp.float32),
            pltpu.SMEM((2, pairs), jnp.int32),
            pltpu.SMEM((1, pairs), jnp.int32),
            pltpu.SMEM((1, pairs), jnp.int32),
            pltpu.SMEM((owners,), jnp.int32),
            pltpu.SMEM((2, groups * groups), jnp.int32),
            pltpu.SemaphoreType.DMA((3,)),
        ],
        compiler_params=pltpu.CompilerParams(vmem_limit_bytes=24 << 20),
        cost_estimate=pl.CostEstimate(
            flops=rows * rows * EXT3, bytes_accessed=2 * rows * EXT3, transcendentals=0
        ),
    )(
        *in_hbm(pair_groups, owner.reshape(1, pairs), owner_slot.reshape(1, pairs)),
        potential,
        far,
        near_total,
    )


def store_kernel(capacity, got, store, total, slots_vector, slots, moved):
    lines = BASIS // 2
    pitch = lines + 1
    sources = got.shape[0]
    stored = store.shape[0]
    for s in range(sources):
        slots_vector[s : s + 1, :] = (
            got[s, capacity * lines : capacity * lines + 8, :].astype(jnp.float32)[:1].astype(jnp.int32)
        )
    copy = pltpu.make_async_copy(slots_vector, slots, moved)
    copy.start()
    total[...] = jnp.zeros_like(total)
    copy.wait()

    def add(s, carry):
        for r in range(capacity):
            at = pl.ds(slots[s, r] * pitch, lines)
            total[at, :] += got[s, r * lines : (r + 1) * lines, :].astype(jnp.float32)
        return carry

    lax.fori_loop(0, sources, add, 0)
    in_low = lax.broadcasted_iota(jnp.int32, (stored, LANES), 1) < BASIS
    for i in range(lines // 2):
        even = total[pl.ds(2 * i, stored, stride=pitch), :]
        odd = total[pl.ds(2 * i + 1, stored, stride=pitch), :]
        for j, row in (
            (i, jnp.where(in_low, even, pltpu.roll(odd, BASIS, axis=1))),
            (i + lines // 2, jnp.where(in_low, pltpu.roll(even, BASIS, axis=1), odd)),
        ):
            store[:, j * LANES : (j + 1) * LANES] = row.astype(store.dtype)


def stored_blocks(got, rows, capacity):
    vmem = pl.BlockSpec(memory_space=pltpu.VMEM)
    return pl.pallas_call(
        functools.partial(store_kernel, capacity),
        name="store",
        out_shape=jax.ShapeDtypeStruct((rows, BASIS * BASIS), jnp.bfloat16),
        in_specs=[vmem],
        out_specs=vmem,
        scratch_shapes=[
            pltpu.VMEM(((rows + 1) * (BASIS // 2 + 1) + 7, LANES), jnp.float32),
            pltpu.VMEM((got.shape[0], LANES), jnp.int32),
            pltpu.SMEM((got.shape[0], LANES), jnp.int32),
            pltpu.SemaphoreType.DMA(()),
        ],
        compiler_params=pltpu.CompilerParams(vmem_limit_bytes=24 << 20),
        cost_estimate=pl.CostEstimate(
            flops=got.size, bytes_accessed=2 * got.size, transcendentals=0
        ),
    )(got)


def per_device(basis, density_blocks, pair_groups, owner, owner_slot):
    pairs = density_blocks.shape[0]
    owners = lax.axis_size("gx") * lax.axis_size("gy")
    capacity = max(2, 2 * pairs // owners)
    groups = basis.shape[0]
    basis = basis.reshape(groups * BASIS, EXT3)
    box, swapped, near_table = collocated(basis, density_blocks, pair_groups)
    box = merged_z(box, swapped, "gz")
    box = jnp.stack(merged(box[0], box[1], "gy"))
    odd, near, far = merged_halves(box[:, : EXT // 2], box[:, EXT // 2 :], "gx")
    near, far = slater_potential(near), slater_potential(far)

    total, far_table = integrated_near(near_table, basis, near)
    send = integrated_far(
        far_table, total, far, pair_groups, owner, owner_slot, owners, capacity
    )
    got = lax.all_to_all(send, ("gx", "gy"), split_axis=0, concat_axis=0, tiled=True)

    potential = jnp.concatenate(
        [jnp.where(odd, near, far)[:, RIM:], jnp.where(odd, far, near)[:, :RIM]], axis=1
    ).reshape(2, CELLS, EXT // 2, EXT)[..., RIM : RIM + CELLS]
    potential = jnp.concatenate([potential[0, :, RIM:], potential[1, :, :RIM]], axis=1)
    return stored_blocks(got, pairs, capacity), potential


def solution(mesh):
    return jax.shard_map(
        per_device,
        mesh=mesh,
        in_specs=(
            P(("gx", "gy", "gz"), None, None),
            P(("gx", "gy", "gz"), None),
            P(None, ("gx", "gy", "gz")),
            P(("gx", "gy", "gz"), None),
            P(("gx", "gy", "gz")),
        ),
        out_specs=(P(("gx", "gy", "gz"), None), P("gx", "gy", "gz")),
        check_vma=False,
    )
```

```python
import functools
import math

import jax
import jax.numpy as jnp
from jax import lax
from jax.experimental import pallas as pl
from jax.experimental.pallas import tpu as pltpu
from jax.sharding import PartitionSpec as P


BASIS = 64
CELLS = 8
RIM = 4
EXT = 16
EXT3 = 4096
LANES = 128

XC_COEF = 0.9847450218426965
GRID_WEIGHT = 0.015625


def slater_potential(density):
    return -XC_COEF * density / jnp.cbrt(density * density + 1.0)


def neighbour_swaps(count, first):
    pairs = []
    for low in range(first, count + first, 2):
        left, right = low % count, (low + 1) % count
        pairs += [(left, right), (right, left)]
    return pairs


def merged_halves(low, high, axis):
    count = lax.axis_size(axis)
    odd = lax.axis_index(axis) % 2 == 1
    near, far = jnp.where(odd, low, high), jnp.where(odd, high, low)
    near = near + lax.ppermute(near, axis, neighbour_swaps(count, 0))
    far = far + lax.ppermute(far, axis, neighbour_swaps(count, 1))
    return odd, near, far


def merged(low, high, axis):
    odd, near, far = merged_halves(low, high, axis)
    return jnp.where(odd, near, far), jnp.where(odd, far, near)


def merged_z(box, swapped, axis):
    count = lax.axis_size(axis)
    if count == 2:
        return box + lax.ppermute(swapped, axis, neighbour_swaps(count, 0))
    odd = lax.axis_index(axis) % 2 == 1
    lane = lax.broadcasted_iota(jnp.int32, box.shape, box.ndim - 1)
    in_high = lane % EXT >= EXT // 2
    first = lax.ppermute(swapped, axis, neighbour_swaps(count, 0))
    second = lax.ppermute(swapped, axis, neighbour_swaps(count, 1))
    return box + jnp.where(in_high != odd, first, second)


def halves():
    odd = lax.axis_index("gx") % 2
    return (1 - odd) * (EXT3 // 2), odd * (EXT3 // 2)


def collocate_kernel(
    groups, pair_groups, blocks, basis, box, swapped, near,
    far, codes, local, spread, matrix, owner_of, arrived, staged,
):
    pairs = blocks.shape[0]
    pitch = BASIS + 1
    codes_copy = pltpu.make_async_copy(pair_groups, codes, staged.at[0])
    blocks_copy = pltpu.make_async_copy(blocks, local, staged.at[1])
    ahead, planes = 2, 4
    cells = planes * EXT * EXT
    copies, plane_of = [], []
    for begin, half in zip(halves(), (near, far)):
        for c in range(half.shape[1] // cells):
            first = pl.multiple_of(begin + c * cells, LANES)
            place = half.at[:, pl.ds(c * cells, cells)]
            copies.append(
                (
                    pltpu.make_async_copy(
                        basis.at[:, pl.ds(first, cells)], place, arrived.at[len(copies)]
                    ),
                    place,
                )
            )
            plane_of.append(begin // (EXT * EXT) + c * planes)
    for copy in [codes_copy, blocks_copy] + [copy for copy, _ in copies[:ahead]]:
        copy.start()
    spread[pl.ds(pairs * pitch, BASIS), :] = jnp.zeros((BASIS, LANES), jnp.float32)
    codes_copy.wait()
    for code in range(groups * groups):
        owner_of[code] = pairs
    for p in range(pairs):
        owner_of[codes[0, p] * groups + codes[1, p]] = p
    blocks_copy.wait()
    in_low = lax.broadcasted_iota(jnp.int32, (pairs, LANES), 1) < BASIS
    for j in range(BASIS // 2):
        two_rows = local[:, j * LANES : (j + 1) * LANES].astype(jnp.float32)
        turned = pltpu.roll(two_rows, BASIS, axis=1)
        spread[pl.ds(2 * j, pairs, stride=pitch), :] = jnp.where(in_low, two_rows, turned)
        spread[pl.ds(2 * j + 1, pairs, stride=pitch), :] = jnp.where(in_low, turned, two_rows)
    left = lax.broadcasted_iota(jnp.int32, (BASIS, LANES), 1) < BASIS
    for first in range(groups):
        for second in range(0, groups, 2):
            code = first * groups + second
            block = spread[pl.ds(owner_of[code] * pitch, BASIS), :]
            if second + 1 < groups:
                block = jnp.where(left, block, spread[pl.ds(owner_of[code + 1] * pitch, BASIS), :])
            matrix[
                first * BASIS : (first + 1) * BASIS, second * BASIS : second * BASIS + LANES
            ] = block.astype(matrix.dtype)
    dense = matrix[:, : groups * BASIS]
    for c, (copy, place) in enumerate(copies):
        copy.wait()
        if c + ahead < len(copies):
            copies[c + ahead][0].start()
        values = place[...]
        projected = jnp.dot(dense, values, preferred_element_type=jnp.float32)
        summed = jnp.sum(values.astype(jnp.float32) * projected, axis=0, keepdims=True)
        for t in range(summed.shape[1] // LANES):
            box[t % 2, pl.ds(plane_of[c] + t // 2, 1), :] = summed[:, t * LANES : (t + 1) * LANES]
    lane = lax.broadcasted_iota(jnp.int32, (EXT, LANES), 1)
    for half in range(2):
        cells = box[half]
        swapped[half] = jnp.where(
            lane % EXT < EXT // 2,
            pltpu.roll(cells, LANES - EXT // 2, axis=1),
            pltpu.roll(cells, EXT // 2, axis=1),
        )


def collocated(basis, density_blocks, pair_groups):
    rows, pairs = basis.shape[0], density_blocks.shape[0]
    groups = rows // BASIS
    vmem, hbm = pl.BlockSpec(memory_space=pltpu.VMEM), pl.BlockSpec(memory_space=pltpu.HBM)
    return pl.pallas_call(
        functools.partial(collocate_kernel, groups),
        name="collocate",
        out_shape=(
            jax.ShapeDtypeStruct((2, EXT, LANES), jnp.float32),
            jax.ShapeDtypeStruct((2, EXT, LANES), jnp.float32),
            jax.ShapeDtypeStruct((rows, EXT3 // 2), basis.dtype),
        ),
        in_specs=[hbm, hbm, hbm],
        out_specs=[vmem, vmem, vmem],
        scratch_shapes=[
            pltpu.VMEM((rows, EXT3 // 2), basis.dtype),
            pltpu.SMEM(pair_groups.shape, jnp.int32),
            pltpu.VMEM(density_blocks.shape, density_blocks.dtype),
            pltpu.VMEM(((pairs + 1) * (BASIS + 1) + 7, LANES), jnp.float32),
            pltpu.VMEM((rows, padded(rows)), jnp.bfloat16),
            pltpu.SMEM((groups * groups,), jnp.int32),
            pltpu.SemaphoreType.DMA((EXT // 2,)),
            pltpu.SemaphoreType.DMA((2,)),
        ],
        compiler_params=pltpu.CompilerParams(vmem_limit_bytes=24 << 20),
        cost_estimate=pl.CostEstimate(
            flops=2 * rows * rows * EXT3, bytes_accessed=2 * rows * EXT3, transcendentals=0
        ),
    )(*in_hbm(pair_groups, density_blocks, basis))


def tabulate(groups, codes, owner, counts, place):
    pairs, owners = codes.shape[1], counts.shape[0]
    lines = BASIS // 2
    for o in range(owners):
        counts[o] = 0
    for code in range(groups * groups):
        place[0, code] = -1
    for p in range(pairs):
        o = owner[0, p]
        rank = counts[o]
        counts[o] = rank + 1
        code = codes[0, p] * groups + codes[1, p]
        place[0, code] = o
        place[1, code] = rank * lines
    free_owner, free_rank = jnp.int32(0), counts[0]
    for o in range(1, owners):
        fewer = counts[o] < free_rank
        free_owner = jnp.where(fewer, o, free_owner)
        free_rank = jnp.where(fewer, counts[o], free_rank)
    for code in range(groups * groups):
        absent = place[0, code] < 0
        place[1, code] = jnp.where(absent, free_rank * lines, place[1, code])
        place[0, code] = jnp.where(absent, free_owner, place[0, code])


def overlaps(table, potential, planes=4):
    cells = planes * EXT * EXT
    for c in range(table.shape[1] // cells):
        values = table[:, c * cells : (c + 1) * cells]
        weight = jnp.concatenate(
            [
                potential[t % 2, planes * c + t // 2 : planes * c + t // 2 + 1, :]
                for t in range(cells // LANES)
            ],
            axis=1,
        )
        weighted = (values.astype(jnp.float32) * weight).astype(jnp.bfloat16)
        yield lax.dot_general(
            weighted, values, (((1,), (1,)), ((), ())), preferred_element_type=jnp.float32
        )


def near_kernel(
    groups, pair_groups, owner, potential, near, basis, total, far, places,
    codes, owners_of, counts, place, arrived, staged,
):
    rows = near.shape[0]
    begin = pl.multiple_of(halves()[1], LANES)
    far_copy = pltpu.make_async_copy(basis.at[:, pl.ds(begin, far.shape[1])], far, arrived)
    codes_copy = pltpu.make_async_copy(pair_groups, codes, staged.at[0])
    owner_copy = pltpu.make_async_copy(owner, owners_of, staged.at[1])
    for copy in (codes_copy, owner_copy, far_copy):
        copy.start()
    for c, part in enumerate(overlaps(near, potential)):
        if c == 0:
            total[:, :rows] = part
            codes_copy.wait()
            owner_copy.wait()
            tabulate(groups, codes, owners_of, counts, place)
        else:
            total[:, :rows] += part
    places_copy = pltpu.make_async_copy(place, places, staged.at[2])
    places_copy.start()
    places_copy.wait()
    far_copy.wait()


def far_kernel(groups, places, potential, far, near_total, send, total, blocks, place, staged, sent):
    rows = groups * BASIS
    lines = BASIS // 2
    places_copy = pltpu.make_async_copy(places, place, staged)
    places_copy.start()
    for c, part in enumerate(overlaps(far, potential)):
        if c == 0:
            total[:, :rows] = near_total[:, :rows] + part
        else:
            total[:, :rows] += part
    places_copy.wait()
    left = lax.broadcasted_iota(jnp.int32, (lines, LANES), 1) < BASIS
    for first in range(groups):
        for second in range(groups):
            code = first * groups + second
            begin = second // 2 * LANES
            upper = total[first * BASIS : first * BASIS + lines, begin : begin + LANES]
            lower = total[first * BASIS + lines : (first + 1) * BASIS, begin : begin + LANES]
            if second % 2 == 0:
                lower = pltpu.roll(lower, BASIS, axis=1)
            else:
                upper = pltpu.roll(upper, BASIS, axis=1)
            blocks[code] = (jnp.where(left, upper, lower) * GRID_WEIGHT).astype(blocks.dtype)
            line = pl.multiple_of(place[1, code], lines)
            pltpu.make_async_copy(
                blocks.at[code], send.at[place[0, code], pl.ds(line, lines), :], sent
            ).start()
    pltpu.make_async_copy(blocks, blocks, sent).wait()


def in_hbm(*arrays):
    return [pltpu.with_memory_space_constraint(x, pltpu.HBM) for x in arrays]


def padded(rows):
    return -(-rows // LANES) * LANES


def integrated_near(near, basis, potential, pair_groups, owner, owners):
    rows, pairs = basis.shape[0], pair_groups.shape[1]
    groups = rows // BASIS
    vmem, hbm = pl.BlockSpec(memory_space=pltpu.VMEM), pl.BlockSpec(memory_space=pltpu.HBM)
    return pl.pallas_call(
        functools.partial(near_kernel, groups),
        name="integrate_near",
        out_shape=(
            jax.ShapeDtypeStruct((rows, padded(rows)), jnp.float32),
            jax.ShapeDtypeStruct((rows, EXT3 // 2), basis.dtype),
            jax.ShapeDtypeStruct((2, groups * groups), jnp.int32),
        ),
        in_specs=[hbm, hbm, vmem, vmem, hbm],
        out_specs=[vmem, vmem, hbm],
        scratch_shapes=[
            pltpu.SMEM((2, pairs), jnp.int32),
            pltpu.SMEM((1, pairs), jnp.int32),
            pltpu.SMEM((owners,), jnp.int32),
            pltpu.SMEM((2, groups * groups), jnp.int32),
            pltpu.SemaphoreType.DMA(()),
            pltpu.SemaphoreType.DMA((3,)),
        ],
        compiler_params=pltpu.CompilerParams(vmem_limit_bytes=24 << 20),
        cost_estimate=pl.CostEstimate(
            flops=rows * rows * EXT3, bytes_accessed=2 * rows * EXT3, transcendentals=0
        ),
    )(*in_hbm(pair_groups, owner.reshape(1, pairs)), potential, near, *in_hbm(basis))


def integrated_far(far, near_total, potential, places, owners, capacity):
    rows = far.shape[0]
    groups = rows // BASIS
    vmem, hbm = pl.BlockSpec(memory_space=pltpu.VMEM), pl.BlockSpec(memory_space=pltpu.HBM)
    return pl.pallas_call(
        functools.partial(far_kernel, groups),
        name="integrate_far",
        out_shape=jax.ShapeDtypeStruct((owners, capacity * BASIS // 2, LANES), jnp.bfloat16),
        in_specs=[hbm, vmem, vmem, vmem],
        out_specs=hbm,
        scratch_shapes=[
            pltpu.VMEM((rows, padded(rows)), jnp.float32),
            pltpu.VMEM((groups * groups, BASIS // 2, LANES), jnp.bfloat16),
            pltpu.SMEM(places.shape, jnp.int32),
            pltpu.SemaphoreType.DMA(()),
            pltpu.SemaphoreType.DMA(()),
        ],
        compiler_params=pltpu.CompilerParams(vmem_limit_bytes=24 << 20),
        cost_estimate=pl.CostEstimate(
            flops=rows * rows * EXT3, bytes_accessed=2 * rows * EXT3, transcendentals=0
        ),
    )(places, potential, far, near_total)


def store_kernel(capacity, got, slot_of, store, total, packed, slots, moved, written):
    lines = BASIS // 2
    pitch = lines + 1
    sources = got.shape[0]
    stored = store.shape[0]
    copy = pltpu.make_async_copy(slot_of, slots, moved)
    copy.start()
    total[...] = jnp.zeros_like(total)
    copy.wait()

    def add(s, carry):
        for r in range(capacity):
            at = pl.ds(slots[s, r] * pitch, lines)
            total[at, :] += got[s, r * lines : (r + 1) * lines, :].astype(jnp.float32)
        return carry

    lax.fori_loop(0, sources, add, 0)
    in_low = lax.broadcasted_iota(jnp.int32, (stored, LANES), 1) < BASIS
    pieces = 4
    span = lines // 2 // pieces
    copies = []
    for piece in range(pieces):
        for i in range(piece * span, (piece + 1) * span):
            even = total[pl.ds(2 * i, stored, stride=pitch), :]
            odd = total[pl.ds(2 * i + 1, stored, stride=pitch), :]
            for j, row in (
                (i, jnp.where(in_low, even, pltpu.roll(odd, BASIS, axis=1))),
                (i + lines // 2, jnp.where(in_low, pltpu.roll(even, BASIS, axis=1), odd)),
            ):
                packed[:, j * LANES : (j + 1) * LANES] = row.astype(packed.dtype)
        for half in range(2):
            columns = pl.ds((half * lines // 2 + piece * span) * LANES, span * LANES)
            copies.append(
                pltpu.make_async_copy(
                    packed.at[:, columns], store.at[:, columns], written.at[len(copies)]
                )
            )
            copies[-1].start()
    for copy in copies:
        copy.wait()


def stored_blocks(got, slot_of, rows, capacity):
    vmem, hbm = pl.BlockSpec(memory_space=pltpu.VMEM), pl.BlockSpec(memory_space=pltpu.HBM)
    return pl.pallas_call(
        functools.partial(store_kernel, capacity),
        name="store",
        out_shape=jax.ShapeDtypeStruct((rows, BASIS * BASIS), jnp.bfloat16),
        in_specs=[vmem, vmem],
        out_specs=hbm,
        scratch_shapes=[
            pltpu.VMEM(((rows + 1) * (BASIS // 2 + 1) + 7, LANES), jnp.float32),
            pltpu.VMEM((rows, BASIS * BASIS), jnp.bfloat16),
            pltpu.SMEM(slot_of.shape, jnp.int32),
            pltpu.SemaphoreType.DMA(()),
            pltpu.SemaphoreType.DMA((8,)),
        ],
        compiler_params=pltpu.CompilerParams(vmem_limit_bytes=24 << 20),
        cost_estimate=pl.CostEstimate(
            flops=got.size, bytes_accessed=2 * got.size, transcendentals=0
        ),
    )(got, slot_of)


def gathered(row, axes):
    sizes = [lax.axis_size(axis) for axis in axes]
    count = math.prod(sizes)
    member = lax.broadcasted_iota(jnp.int32, (count, row.shape[-1]), 0)
    table = jnp.where(member == lax.axis_index(axes), row[None, :], 0.0)
    for axis, size in zip(axes[::-1], sizes[::-1]):
        step = 1
        while step < size:
            other = lax.ppermute(table, axis, [(i, i ^ step) for i in range(size)])
            table = table + other
            step *= 2
    return table


def slots_of_sources(owner, owner_slot, axes):
    pairs = owner_slot.shape[0]
    named = jnp.pad((owner[:, 0] * pairs + owner_slot + 1).astype(jnp.float32), (0, LANES - pairs))
    named = gathered(named, axes)[:, :pairs].astype(jnp.int32) - 1
    slot = named - lax.axis_index(axes) * pairs
    mine = (slot >= 0) & (slot < pairs)
    order = jnp.arange(pairs, dtype=jnp.int32)
    before = mine[:, None, :] & (order[None, None, :] < order[None, :, None])
    rank = jnp.where(mine, jnp.sum(before.astype(jnp.int32), axis=2), -1)
    at_rank = rank[:, None, :] == jnp.arange(LANES, dtype=jnp.int32)[None, :, None]
    return jnp.sum(jnp.where(at_rank, slot[:, None, :] - pairs, 0), axis=2) + pairs


def per_device(basis, density_blocks, pair_groups, owner, owner_slot):
    pairs = density_blocks.shape[0]
    owners = lax.axis_size("gx") * lax.axis_size("gy")
    capacity = max(2, 2 * pairs // owners)
    groups = basis.shape[0]
    basis = basis.reshape(groups * BASIS, EXT3)
    box, swapped, near_table = collocated(basis, density_blocks, pair_groups)
    box = merged_z(box, swapped, "gz")
    box = jnp.stack(merged(box[0], box[1], "gy"))
    odd, near, far = merged_halves(box[:, : EXT // 2], box[:, EXT // 2 :], "gx")
    near, far = slater_potential(near), slater_potential(far)

    total, far_table, places = integrated_near(
        near_table, basis, near, pair_groups, owner, owners
    )
    send = integrated_far(far_table, total, far, places, owners, capacity)
    send, late_owner, late_slot = lax.optimization_barrier((send, owner, owner_slot))
    got = lax.all_to_all(send, ("gx", "gy"), split_axis=0, concat_axis=0, tiled=True)
    slot_of = slots_of_sources(late_owner, late_slot, ("gx", "gy"))

    potential = jnp.concatenate(
        [jnp.where(odd, near, far)[:, RIM:], jnp.where(odd, far, near)[:, :RIM]], axis=1
    ).reshape(2, CELLS, EXT // 2, EXT)[..., RIM : RIM + CELLS]
    potential = jnp.concatenate([potential[0, :, RIM:], potential[1, :, :RIM]], axis=1)
    return stored_blocks(got, slot_of, pairs, capacity), potential


def solution(mesh):
    return jax.shard_map(
        per_device,
        mesh=mesh,
        in_specs=(
            P(("gx", "gy", "gz"), None, None),
            P(("gx", "gy", "gz"), None),
            P(None, ("gx", "gy", "gz")),
            P(("gx", "gy", "gz"), None),
            P(("gx", "gy", "gz")),
        ),
        out_specs=(P(("gx", "gy", "gz"), None), P("gx", "gy", "gz")),
        check_vma=False,
    )
```

```python
import functools

import jax
import jax.numpy as jnp
from jax import lax
from jax.experimental import pallas as pl
from jax.experimental.pallas import tpu as pltpu
from jax.sharding import PartitionSpec as P

BASIS = 64
CELLS = 8
RIM = 4
EXT = 16
EXT3 = 4096
LANES = 128

XC_COEF = 0.9847450218426965
GRID_WEIGHT = 0.015625


def slater_potential(density):
    return -XC_COEF * density / jnp.cbrt(density * density + 1.0)


def neighbour_swaps(count, first):
    pairs = []
    for low in range(first, count + first, 2):
        left, right = low % count, (low + 1) % count
        pairs += [(left, right), (right, left)]
    return pairs


def merged_halves(low, high, axis):
    count = lax.axis_size(axis)
    odd = lax.axis_index(axis) % 2 == 1
    near, far = jnp.where(odd, low, high), jnp.where(odd, high, low)
    near = near + lax.ppermute(near, axis, neighbour_swaps(count, 0))
    far = far + lax.ppermute(far, axis, neighbour_swaps(count, 1))
    return odd, near, far


def merged(low, high, axis):
    odd, near, far = merged_halves(low, high, axis)
    return jnp.where(odd, near, far), jnp.where(odd, far, near)


def merged_z(box, swapped, axis):
    count = lax.axis_size(axis)
    if count == 2:
        return box + lax.ppermute(swapped, axis, neighbour_swaps(count, 0))
    odd = lax.axis_index(axis) % 2 == 1
    lane = lax.broadcasted_iota(jnp.int32, box.shape, box.ndim - 1)
    in_high = lane % EXT >= EXT // 2
    first = lax.ppermute(swapped, axis, neighbour_swaps(count, 0))
    second = lax.ppermute(swapped, axis, neighbour_swaps(count, 1))
    return box + jnp.where(in_high != odd, first, second)


def halves():
    odd = lax.axis_index("gx") % 2
    return (1 - odd) * (EXT3 // 2), odd * (EXT3 // 2)


def collocate_kernel(
    groups, pair_groups, blocks, basis, box, swapped, near,
    far, codes, local, spread, matrix, owner_of, arrived, staged,
):
    pairs = blocks.shape[0]
    pitch = BASIS + 1
    codes_copy = pltpu.make_async_copy(pair_groups, codes, staged.at[0])
    blocks_copy = pltpu.make_async_copy(blocks, local, staged.at[1])
    ahead, planes = 2, 4
    cells = planes * EXT * EXT
    copies, plane_of = [], []
    for begin, half in zip(halves(), (near, far)):
        for c in range(half.shape[1] // cells):
            first = pl.multiple_of(begin + c * cells, LANES)
            place = half.at[:, pl.ds(c * cells, cells)]
            copies.append(
                (
                    pltpu.make_async_copy(
                        basis.at[:, pl.ds(first, cells)], place, arrived.at[len(copies)]
                    ),
                    place,
                )
            )
            plane_of.append(begin // (EXT * EXT) + c * planes)
    for copy in [codes_copy, blocks_copy] + [copy for copy, _ in copies[:ahead]]:
        copy.start()
    spread[pl.ds(pairs * pitch, BASIS), :] = jnp.zeros((BASIS, LANES), jnp.float32)
    codes_copy.wait()
    for code in range(groups * groups):
        owner_of[code] = pairs
    for p in range(pairs):
        owner_of[codes[0, p] * groups + codes[1, p]] = p
    blocks_copy.wait()
    in_low = lax.broadcasted_iota(jnp.int32, (pairs, LANES), 1) < BASIS
    for j in range(BASIS // 2):
        two_rows = local[:, j * LANES : (j + 1) * LANES].astype(jnp.float32)
        turned = pltpu.roll(two_rows, BASIS, axis=1)
        spread[pl.ds(2 * j, pairs, stride=pitch), :] = jnp.where(in_low, two_rows, turned)
        spread[pl.ds(2 * j + 1, pairs, stride=pitch), :] = jnp.where(in_low, turned, two_rows)
    left = lax.broadcasted_iota(jnp.int32, (BASIS, LANES), 1) < BASIS
    for first in range(groups):
        for second in range(0, groups, 2):
            code = first * groups + second
            block = spread[pl.ds(owner_of[code] * pitch, BASIS), :]
            if second + 1 < groups:
                block = jnp.where(left, block, spread[pl.ds(owner_of[code + 1] * pitch, BASIS), :])
            matrix[
                first * BASIS : (first + 1) * BASIS, second * BASIS : second * BASIS + LANES
            ] = block.astype(matrix.dtype)
    dense = matrix[:, : groups * BASIS]
    for c, (copy, place) in enumerate(copies):
        copy.wait()
        if c + ahead < len(copies):
            copies[c + ahead][0].start()
        values = place[...]
        projected = jnp.dot(dense, values, preferred_element_type=jnp.float32)
        summed = jnp.sum(values.astype(jnp.float32) * projected, axis=0, keepdims=True)
        for t in range(summed.shape[1] // LANES):
            box[t % 2, pl.ds(plane_of[c] + t // 2, 1), :] = summed[:, t * LANES : (t + 1) * LANES]
    lane = lax.broadcasted_iota(jnp.int32, (EXT, LANES), 1)
    for half in range(2):
        cells = box[half]
        swapped[half] = jnp.where(
            lane % EXT < EXT // 2,
            pltpu.roll(cells, LANES - EXT // 2, axis=1),
            pltpu.roll(cells, EXT // 2, axis=1),
        )


def collocated(basis, density_blocks, pair_groups):
    rows, pairs = basis.shape[0], density_blocks.shape[0]
    groups = rows // BASIS
    vmem, hbm = pl.BlockSpec(memory_space=pltpu.VMEM), pl.BlockSpec(memory_space=pltpu.HBM)
    return pl.pallas_call(
        functools.partial(collocate_kernel, groups),
        name="collocate",
        out_shape=(
            jax.ShapeDtypeStruct((2, EXT, LANES), jnp.float32),
            jax.ShapeDtypeStruct((2, EXT, LANES), jnp.float32),
            jax.ShapeDtypeStruct((rows, EXT3 // 2), basis.dtype),
        ),
        in_specs=[hbm, hbm, hbm],
        out_specs=[vmem, vmem, vmem],
        scratch_shapes=[
            pltpu.VMEM((rows, EXT3 // 2), basis.dtype),
            pltpu.SMEM(pair_groups.shape, jnp.int32),
            pltpu.VMEM(density_blocks.shape, density_blocks.dtype),
            pltpu.VMEM(((pairs + 1) * (BASIS + 1) + 7, LANES), jnp.float32),
            pltpu.VMEM((rows, padded(rows)), jnp.bfloat16),
            pltpu.SMEM((groups * groups,), jnp.int32),
            pltpu.SemaphoreType.DMA((EXT // 2,)),
            pltpu.SemaphoreType.DMA((2,)),
        ],
        compiler_params=pltpu.CompilerParams(vmem_limit_bytes=24 << 20),
        cost_estimate=pl.CostEstimate(
            flops=2 * rows * rows * EXT3, bytes_accessed=2 * rows * EXT3, transcendentals=0
        ),
    )(*in_hbm(pair_groups, density_blocks, basis))


def tabulate(groups, codes, owner, slot, counts, place, slot_rows):
    pairs, owners = codes.shape[1], counts.shape[0]
    lines = BASIS // 2
    slot_rows[...] = jnp.full(slot_rows.shape, pairs, jnp.float32)
    lane = lax.broadcasted_iota(jnp.int32, (1, LANES), 1)
    for o in range(owners):
        counts[o] = 0
    for code in range(groups * groups):
        place[0, code] = -1
    for p in range(pairs):
        o = owner[0, p]
        rank = counts[o]
        counts[o] = rank + 1
        code = codes[0, p] * groups + codes[1, p]
        place[0, code] = o
        place[1, code] = rank * lines
        row = slot_rows[pl.ds(o, 1), :]
        slot_rows[pl.ds(o, 1), :] = jnp.where(lane == rank, slot[0, p].astype(jnp.float32), row)
    free_owner, free_rank = jnp.int32(0), counts[0]
    for o in range(1, owners):
        fewer = counts[o] < free_rank
        free_owner = jnp.where(fewer, o, free_owner)
        free_rank = jnp.where(fewer, counts[o], free_rank)
    for code in range(groups * groups):
        absent = place[0, code] < 0
        place[1, code] = jnp.where(absent, free_rank * lines, place[1, code])
        place[0, code] = jnp.where(absent, free_owner, place[0, code])


def overlaps(table, potential, planes=4):
    cells = planes * EXT * EXT
    for c in range(table.shape[1] // cells):
        values = table[:, c * cells : (c + 1) * cells]
        weight = jnp.concatenate(
            [
                potential[t % 2, planes * c + t // 2 : planes * c + t // 2 + 1, :]
                for t in range(cells // LANES)
            ],
            axis=1,
        )
        weighted = (values.astype(jnp.float32) * weight).astype(jnp.bfloat16)
        yield lax.dot_general(
            weighted, values, (((1,), (1,)), ((), ())), preferred_element_type=jnp.float32
        )


def near_kernel(
    groups, pair_groups, owner, owner_slot, potential, near, basis, total, far, places, slots,
    codes, owners_of, slots_of, counts, place, slot_rows, arrived, staged,
):
    rows = near.shape[0]
    begin = pl.multiple_of(halves()[1], LANES)
    far_copy = pltpu.make_async_copy(basis.at[:, pl.ds(begin, far.shape[1])], far, arrived)
    tables = [
        pltpu.make_async_copy(source, target, staged.at[i])
        for i, (source, target) in enumerate(
            [(pair_groups, codes), (owner, owners_of), (owner_slot, slots_of)]
        )
    ]
    for copy in tables + [far_copy]:
        copy.start()
    for c, part in enumerate(overlaps(near, potential)):
        if c == 0:
            total[:, :rows] = part
            for copy in tables:
                copy.wait()
            tabulate(groups, codes, owners_of, slots_of, counts, place, slot_rows)
        else:
            total[:, :rows] += part
    places_copy = pltpu.make_async_copy(place, places, staged.at[3])
    places_copy.start()
    for o in range(slots.shape[0]):
        slots[o] = jnp.broadcast_to(slot_rows[o : o + 1, :], slots.shape[1:]).astype(slots.dtype)
    places_copy.wait()
    far_copy.wait()


def far_kernel(
    groups, places, slots, potential, far, near_total, send, total, blocks, place, staged, sent
):
    rows = groups * BASIS
    lines = BASIS // 2
    places_copy = pltpu.make_async_copy(places, place, staged.at[0])
    slots_copy = pltpu.make_async_copy(
        slots, send.at[:, pl.ds(send.shape[1] - slots.shape[1], slots.shape[1]), :], staged.at[1]
    )
    places_copy.start()
    slots_copy.start()
    for c, part in enumerate(overlaps(far, potential)):
        if c == 0:
            total[:, :rows] = near_total[:, :rows] + part
        else:
            total[:, :rows] += part
    places_copy.wait()
    left = lax.broadcasted_iota(jnp.int32, (lines, LANES), 1) < BASIS
    for first in range(groups):
        for second in range(groups):
            code = first * groups + second
            begin = second // 2 * LANES
            upper = total[first * BASIS : first * BASIS + lines, begin : begin + LANES]
            lower = total[first * BASIS + lines : (first + 1) * BASIS, begin : begin + LANES]
            if second % 2 == 0:
                lower = pltpu.roll(lower, BASIS, axis=1)
            else:
                upper = pltpu.roll(upper, BASIS, axis=1)
            blocks[code] = (jnp.where(left, upper, lower) * GRID_WEIGHT).astype(blocks.dtype)
            line = pl.multiple_of(place[1, code], lines)
            pltpu.make_async_copy(
                blocks.at[code], send.at[place[0, code], pl.ds(line, lines), :], sent
            ).start()
    slots_copy.wait()
    pltpu.make_async_copy(blocks, blocks, sent).wait()


def in_hbm(*arrays):
    return [pltpu.with_memory_space_constraint(x, pltpu.HBM) for x in arrays]


def padded(rows):
    return -(-rows // LANES) * LANES


def integrated_near(near, basis, potential, pair_groups, owner, owner_slot, owners):
    rows, pairs = basis.shape[0], pair_groups.shape[1]
    groups = rows // BASIS
    vmem, hbm = pl.BlockSpec(memory_space=pltpu.VMEM), pl.BlockSpec(memory_space=pltpu.HBM)
    return pl.pallas_call(
        functools.partial(near_kernel, groups),
        name="integrate_near",
        out_shape=(
            jax.ShapeDtypeStruct((rows, padded(rows)), jnp.float32),
            jax.ShapeDtypeStruct((rows, EXT3 // 2), basis.dtype),
            jax.ShapeDtypeStruct((2, groups * groups), jnp.int32),
            jax.ShapeDtypeStruct((owners, 8, LANES), jnp.bfloat16),
        ),
        in_specs=[hbm, hbm, hbm, vmem, vmem, hbm],
        out_specs=[vmem, vmem, hbm, vmem],
        scratch_shapes=[
            pltpu.SMEM((2, pairs), jnp.int32),
            pltpu.SMEM((1, pairs), jnp.int32),
            pltpu.SMEM((1, pairs), jnp.int32),
            pltpu.SMEM((owners,), jnp.int32),
            pltpu.SMEM((2, groups * groups), jnp.int32),
            pltpu.VMEM((owners, LANES), jnp.float32),
            pltpu.SemaphoreType.DMA(()),
            pltpu.SemaphoreType.DMA((4,)),
        ],
        compiler_params=pltpu.CompilerParams(vmem_limit_bytes=24 << 20),
        cost_estimate=pl.CostEstimate(
            flops=rows * rows * EXT3, bytes_accessed=2 * rows * EXT3, transcendentals=0
        ),
    )(
        *in_hbm(pair_groups, owner.reshape(1, pairs), owner_slot.reshape(1, pairs)),
        potential,
        near,
        *in_hbm(basis),
    )


def integrated_far(far, near_total, potential, places, slots, capacity):
    rows = far.shape[0]
    groups = rows // BASIS
    vmem, hbm = pl.BlockSpec(memory_space=pltpu.VMEM), pl.BlockSpec(memory_space=pltpu.HBM)
    return pl.pallas_call(
        functools.partial(far_kernel, groups),
        name="integrate_far",
        out_shape=jax.ShapeDtypeStruct(
            (slots.shape[0], capacity * BASIS // 2 + slots.shape[1], LANES), jnp.bfloat16
        ),
        in_specs=[hbm, vmem, vmem, vmem, vmem],
        out_specs=hbm,
        scratch_shapes=[
            pltpu.VMEM((rows, padded(rows)), jnp.float32),
            pltpu.VMEM((groups * groups, BASIS // 2, LANES), jnp.bfloat16),
            pltpu.SMEM(places.shape, jnp.int32),
            pltpu.SemaphoreType.DMA((2,)),
            pltpu.SemaphoreType.DMA(()),
        ],
        compiler_params=pltpu.CompilerParams(vmem_limit_bytes=24 << 20),
        cost_estimate=pl.CostEstimate(
            flops=rows * rows * EXT3, bytes_accessed=2 * rows * EXT3, transcendentals=0
        ),
    )(places, slots, potential, far, near_total)


def store_kernel(capacity, got, store, total, packed, written):
    lines = BASIS // 2
    pitch = lines + 1
    stored = store.shape[0]
    total[...] = jnp.zeros_like(total)
    for s in range(got.shape[0]):
        slots = got[s, capacity * lines : capacity * lines + 8, :].astype(jnp.float32)
        slots = slots[:1].astype(jnp.int32)
        for r in range(capacity):
            at = pl.ds(slots[0, r] * pitch, lines)
            total[at, :] += got[s, r * lines : (r + 1) * lines, :].astype(jnp.float32)
    in_low = lax.broadcasted_iota(jnp.int32, (stored, LANES), 1) < BASIS
    pieces = 4
    span = lines // 2 // pieces
    copies = []
    for piece in range(pieces):
        for i in range(piece * span, (piece + 1) * span):
            even = total[pl.ds(2 * i, stored, stride=pitch), :]
            odd = total[pl.ds(2 * i + 1, stored, stride=pitch), :]
            for j, row in (
                (i, jnp.where(in_low, even, pltpu.roll(odd, BASIS, axis=1))),
                (i + lines // 2, jnp.where(in_low, pltpu.roll(even, BASIS, axis=1), odd)),
            ):
                packed[:, j * LANES : (j + 1) * LANES] = row.astype(packed.dtype)
        for half in range(2):
            columns = pl.ds((half * lines // 2 + piece * span) * LANES, span * LANES)
            copies.append(
                pltpu.make_async_copy(
                    packed.at[:, columns], store.at[:, columns], written.at[len(copies)]
                )
            )
            copies[-1].start()
    for copy in copies:
        copy.wait()


def stored_blocks(got, rows, capacity):
    vmem, hbm = pl.BlockSpec(memory_space=pltpu.VMEM), pl.BlockSpec(memory_space=pltpu.HBM)
    return pl.pallas_call(
        functools.partial(store_kernel, capacity),
        name="store",
        out_shape=jax.ShapeDtypeStruct((rows, BASIS * BASIS), jnp.bfloat16),
        in_specs=[vmem],
        out_specs=hbm,
        scratch_shapes=[
            pltpu.VMEM(((rows + 1) * (BASIS // 2 + 1) + 7, LANES), jnp.float32),
            pltpu.VMEM((rows, BASIS * BASIS), jnp.bfloat16),
            pltpu.SemaphoreType.DMA((8,)),
        ],
        compiler_params=pltpu.CompilerParams(vmem_limit_bytes=24 << 20),
        cost_estimate=pl.CostEstimate(
            flops=got.size, bytes_accessed=2 * got.size, transcendentals=0
        ),
    )(got)


def per_device(basis, density_blocks, pair_groups, owner, owner_slot):
    pairs = density_blocks.shape[0]
    owners = lax.axis_size("gx") * lax.axis_size("gy")
    capacity = max(2, 2 * pairs // owners)
    groups = basis.shape[0]
    basis = basis.reshape(groups * BASIS, EXT3)
    box, swapped, near_table = collocated(basis, density_blocks, pair_groups)
    box = merged_z(box, swapped, "gz")
    box = jnp.stack(merged(box[0], box[1], "gy"))
    odd, near, far = merged_halves(box[:, : EXT // 2], box[:, EXT // 2 :], "gx")
    near, far = slater_potential(near), slater_potential(far)

    total, far_table, places, slots = integrated_near(
        near_table, basis, near, pair_groups, owner, owner_slot, owners
    )
    send = integrated_far(far_table, total, far, places, slots, capacity)
    got = lax.all_to_all(send, ("gx", "gy"), split_axis=0, concat_axis=0, tiled=True)

    potential = jnp.concatenate(
        [jnp.where(odd, near, far)[:, RIM:], jnp.where(odd, far, near)[:, :RIM]], axis=1
    ).reshape(2, CELLS, EXT // 2, EXT)[..., RIM : RIM + CELLS]
    potential = jnp.concatenate([potential[0, :, RIM:], potential[1, :, :RIM]], axis=1)
    return stored_blocks(got, pairs, capacity), potential


def solution(mesh):
    return jax.shard_map(
        per_device,
        mesh=mesh,
        in_specs=(
            P(("gx", "gy", "gz"), None, None),
            P(("gx", "gy", "gz"), None),
            P(None, ("gx", "gy", "gz")),
            P(("gx", "gy", "gz"), None),
            P(("gx", "gy", "gz")),
        ),
        out_specs=(P(("gx", "gy", "gz"), None), P("gx", "gy", "gz")),
        check_vma=False,
    )
```

```python
import functools

import jax
import jax.numpy as jnp
from jax import lax
from jax.experimental import pallas as pl
from jax.experimental.pallas import tpu as pltpu
from jax.sharding import PartitionSpec as P

BASIS = 64
CELLS = 8
RIM = 4
EXT = 16
EXT3 = 4096
LANES = 128

XC_COEF = 0.9847450218426965
GRID_WEIGHT = 0.015625


def slater_potential(density):
    return -XC_COEF * density / jnp.cbrt(density * density + 1.0)


def neighbour_swaps(count, first):
    pairs = []
    for low in range(first, count + first, 2):
        left, right = low % count, (low + 1) % count
        pairs += [(left, right), (right, left)]
    return pairs


def merged_halves(low, high, axis):
    count = lax.axis_size(axis)
    odd = lax.axis_index(axis) % 2 == 1
    near, far = jnp.where(odd, low, high), jnp.where(odd, high, low)
    near = near + lax.ppermute(near, axis, neighbour_swaps(count, 0))
    far = far + lax.ppermute(far, axis, neighbour_swaps(count, 1))
    return odd, near, far


def merged(low, high, axis):
    odd, near, far = merged_halves(low, high, axis)
    return jnp.where(odd, near, far), jnp.where(odd, far, near)


def merged_z(box, swapped, axis):
    count = lax.axis_size(axis)
    if count == 2:
        return box + lax.ppermute(swapped, axis, neighbour_swaps(count, 0))
    odd = lax.axis_index(axis) % 2 == 1
    lane = lax.broadcasted_iota(jnp.int32, box.shape, box.ndim - 1)
    in_high = lane % EXT >= EXT // 2
    first = lax.ppermute(swapped, axis, neighbour_swaps(count, 0))
    second = lax.ppermute(swapped, axis, neighbour_swaps(count, 1))
    return box + jnp.where(in_high != odd, first, second)


def halves():
    odd = lax.axis_index("gx") % 2
    return (1 - odd) * (EXT3 // 2), odd * (EXT3 // 2)


def collocate_kernel(
    groups, pair_groups, blocks, basis, box, swapped, near,
    far, codes, local, spread, matrix, owner_of, arrived, staged,
):
    pairs = blocks.shape[0]
    pitch = BASIS + 1
    codes_copy = pltpu.make_async_copy(pair_groups, codes, staged.at[0])
    blocks_copy = pltpu.make_async_copy(blocks, local, staged.at[1])
    ahead, planes = 2, 4
    cells = planes * EXT * EXT
    copies, plane_of = [], []
    for begin, half in zip(halves(), (near, far)):
        for c in range(half.shape[1] // cells):
            first = pl.multiple_of(begin + c * cells, LANES)
            place = half.at[:, pl.ds(c * cells, cells)]
            copies.append(
                (
                    pltpu.make_async_copy(
                        basis.at[:, pl.ds(first, cells)], place, arrived.at[len(copies)]
                    ),
                    place,
                )
            )
            plane_of.append(begin // (EXT * EXT) + c * planes)
    for copy in [codes_copy, blocks_copy] + [copy for copy, _ in copies[:ahead]]:
        copy.start()
    spread[pl.ds(pairs * pitch, BASIS), :] = jnp.zeros((BASIS, LANES), jnp.float32)
    codes_copy.wait()
    for code in range(groups * groups):
        owner_of[code] = pairs
    for p in range(pairs):
        owner_of[codes[0, p] * groups + codes[1, p]] = p
    blocks_copy.wait()
    in_low = lax.broadcasted_iota(jnp.int32, (pairs, LANES), 1) < BASIS
    for j in range(BASIS // 2):
        two_rows = local[:, j * LANES : (j + 1) * LANES].astype(jnp.float32)
        turned = pltpu.roll(two_rows, BASIS, axis=1)
        spread[pl.ds(2 * j, pairs, stride=pitch), :] = jnp.where(in_low, two_rows, turned)
        spread[pl.ds(2 * j + 1, pairs, stride=pitch), :] = jnp.where(in_low, turned, two_rows)
    left = lax.broadcasted_iota(jnp.int32, (BASIS, LANES), 1) < BASIS
    for first in range(groups):
        for second in range(0, groups, 2):
            code = first * groups + second
            block = spread[pl.ds(owner_of[code] * pitch, BASIS), :]
            if second + 1 < groups:
                block = jnp.where(left, block, spread[pl.ds(owner_of[code + 1] * pitch, BASIS), :])
            matrix[
                first * BASIS : (first + 1) * BASIS, second * BASIS : second * BASIS + LANES
            ] = block.astype(matrix.dtype)
    dense = matrix[:, : groups * BASIS]
    for c, (copy, place) in enumerate(copies):
        copy.wait()
        if c + ahead < len(copies):
            copies[c + ahead][0].start()
        values = place[...]
        projected = jnp.dot(dense, values, preferred_element_type=jnp.float32)
        summed = jnp.sum(values.astype(jnp.float32) * projected, axis=0, keepdims=True)
        for t in range(summed.shape[1] // LANES):
            box[t % 2, pl.ds(plane_of[c] + t // 2, 1), :] = summed[:, t * LANES : (t + 1) * LANES]
    lane = lax.broadcasted_iota(jnp.int32, (EXT, LANES), 1)
    for half in range(2):
        cells = box[half]
        swapped[half] = jnp.where(
            lane % EXT < EXT // 2,
            pltpu.roll(cells, LANES - EXT // 2, axis=1),
            pltpu.roll(cells, EXT // 2, axis=1),
        )


def collocated(basis, density_blocks, pair_groups):
    rows, pairs = basis.shape[0], density_blocks.shape[0]
    groups = rows // BASIS
    vmem, hbm = pl.BlockSpec(memory_space=pltpu.VMEM), pl.BlockSpec(memory_space=pltpu.HBM)
    return pl.pallas_call(
        functools.partial(collocate_kernel, groups),
        name="collocate",
        out_shape=(
            jax.ShapeDtypeStruct((2, EXT, LANES), jnp.float32),
            jax.ShapeDtypeStruct((2, EXT, LANES), jnp.float32),
            jax.ShapeDtypeStruct((rows, EXT3 // 2), basis.dtype),
        ),
        in_specs=[hbm, hbm, hbm],
        out_specs=[vmem, vmem, vmem],
        scratch_shapes=[
            pltpu.VMEM((rows, EXT3 // 2), basis.dtype),
            pltpu.SMEM(pair_groups.shape, jnp.int32),
            pltpu.VMEM(density_blocks.shape, density_blocks.dtype),
            pltpu.VMEM(((pairs + 1) * (BASIS + 1) + 7, LANES), jnp.float32),
            pltpu.VMEM((rows, padded(rows)), jnp.bfloat16),
            pltpu.SMEM((groups * groups,), jnp.int32),
            pltpu.SemaphoreType.DMA((EXT // 2,)),
            pltpu.SemaphoreType.DMA((2,)),
        ],
        compiler_params=pltpu.CompilerParams(vmem_limit_bytes=24 << 20),
        cost_estimate=pl.CostEstimate(
            flops=2 * rows * rows * EXT3, bytes_accessed=2 * rows * EXT3, transcendentals=0
        ),
    )(*in_hbm(pair_groups, density_blocks, basis))


def tabulate(groups, codes, owner, slot, counts, place, slot_rows):
    pairs, owners = codes.shape[1], counts.shape[0]
    lines = BASIS // 2
    slot_rows[...] = jnp.full(slot_rows.shape, pairs, jnp.float32)
    lane = lax.broadcasted_iota(jnp.int32, (1, LANES), 1)
    for o in range(owners):
        counts[o] = 0
    for code in range(groups * groups):
        place[0, code] = -1
    for p in range(pairs):
        o = owner[0, p]
        rank = counts[o]
        counts[o] = rank + 1
        code = codes[0, p] * groups + codes[1, p]
        place[0, code] = o
        place[1, code] = rank * lines
        row = slot_rows[pl.ds(o, 1), :]
        slot_rows[pl.ds(o, 1), :] = jnp.where(lane == rank, slot[0, p].astype(jnp.float32), row)
    free_owner, free_rank = jnp.int32(0), counts[0]
    for o in range(1, owners):
        fewer = counts[o] < free_rank
        free_owner = jnp.where(fewer, o, free_owner)
        free_rank = jnp.where(fewer, counts[o], free_rank)
    for code in range(groups * groups):
        absent = place[0, code] < 0
        place[1, code] = jnp.where(absent, free_rank * lines, place[1, code])
        place[0, code] = jnp.where(absent, free_owner, place[0, code])


def overlaps(table, potential, planes=4):
    cells = planes * EXT * EXT
    for c in range(table.shape[1] // cells):
        values = table[:, c * cells : (c + 1) * cells]
        weight = jnp.concatenate(
            [
                potential[t % 2, planes * c + t // 2 : planes * c + t // 2 + 1, :]
                for t in range(cells // LANES)
            ],
            axis=1,
        )
        weighted = (values.astype(jnp.float32) * weight).astype(jnp.bfloat16)
        yield lax.dot_general(
            weighted, values, (((1,), (1,)), ((), ())), preferred_element_type=jnp.float32
        )


def near_kernel(
    groups, pair_groups, owner, owner_slot, potential, near, basis, total, far, places, slots,
    codes, owners_of, slots_of, counts, place, slot_rows, arrived, staged,
):
    rows = near.shape[0]
    begin = pl.multiple_of(halves()[1], LANES)
    far_copy = pltpu.make_async_copy(basis.at[:, pl.ds(begin, far.shape[1])], far, arrived)
    tables = [
        pltpu.make_async_copy(source, target, staged.at[i])
        for i, (source, target) in enumerate(
            [(pair_groups, codes), (owner, owners_of), (owner_slot, slots_of)]
        )
    ]
    for copy in tables + [far_copy]:
        copy.start()
    for c, part in enumerate(overlaps(near, potential)):
        if c == 0:
            total[:, :rows] = part
            for copy in tables:
                copy.wait()
            tabulate(groups, codes, owners_of, slots_of, counts, place, slot_rows)
        else:
            total[:, :rows] += part
    places_copy = pltpu.make_async_copy(place, places, staged.at[3])
    places_copy.start()
    for o in range(slots.shape[0]):
        slots[o] = jnp.broadcast_to(slot_rows[o : o + 1, :], slots.shape[1:]).astype(slots.dtype)
    places_copy.wait()
    far_copy.wait()


def far_kernel(
    groups, places, slots, potential, far, near_total, send, total, blocks, place, staged, sent
):
    rows = groups * BASIS
    lines = BASIS // 2
    places_copy = pltpu.make_async_copy(places, place, staged.at[0])
    slots_copy = pltpu.make_async_copy(
        slots, send.at[:, pl.ds(send.shape[1] - slots.shape[1], slots.shape[1]), :], staged.at[1]
    )
    places_copy.start()
    slots_copy.start()
    for c, part in enumerate(overlaps(far, potential)):
        if c == 0:
            total[:, :rows] = near_total[:, :rows] + part
        else:
            total[:, :rows] += part
    places_copy.wait()
    left = lax.broadcasted_iota(jnp.int32, (lines, LANES), 1) < BASIS
    for first in range(groups):
        for second in range(groups):
            code = first * groups + second
            begin = second // 2 * LANES
            upper = total[first * BASIS : first * BASIS + lines, begin : begin + LANES]
            lower = total[first * BASIS + lines : (first + 1) * BASIS, begin : begin + LANES]
            if second % 2 == 0:
                lower = pltpu.roll(lower, BASIS, axis=1)
            else:
                upper = pltpu.roll(upper, BASIS, axis=1)
            blocks[code] = (jnp.where(left, upper, lower) * GRID_WEIGHT).astype(blocks.dtype)
            line = pl.multiple_of(place[1, code], lines)
            pltpu.make_async_copy(
                blocks.at[code], send.at[place[0, code], pl.ds(line, lines), :], sent
            ).start()
    slots_copy.wait()
    pltpu.make_async_copy(blocks, blocks, sent).wait()


def in_hbm(*arrays):
    return [pltpu.with_memory_space_constraint(x, pltpu.HBM) for x in arrays]


def padded(rows):
    return -(-rows // LANES) * LANES


def integrated_near(near, basis, potential, pair_groups, owner, owner_slot, owners):
    rows, pairs = basis.shape[0], pair_groups.shape[1]
    groups = rows // BASIS
    vmem, hbm = pl.BlockSpec(memory_space=pltpu.VMEM), pl.BlockSpec(memory_space=pltpu.HBM)
    return pl.pallas_call(
        functools.partial(near_kernel, groups),
        name="integrate_near",
        out_shape=(
            jax.ShapeDtypeStruct((rows, padded(rows)), jnp.float32),
            jax.ShapeDtypeStruct((rows, EXT3 // 2), basis.dtype),
            jax.ShapeDtypeStruct((2, groups * groups), jnp.int32),
            jax.ShapeDtypeStruct((owners, 8, LANES), jnp.bfloat16),
        ),
        in_specs=[hbm, hbm, hbm, vmem, vmem, hbm],
        out_specs=[vmem, vmem, hbm, vmem],
        scratch_shapes=[
            pltpu.SMEM((2, pairs), jnp.int32),
            pltpu.SMEM((1, pairs), jnp.int32),
            pltpu.SMEM((1, pairs), jnp.int32),
            pltpu.SMEM((owners,), jnp.int32),
            pltpu.SMEM((2, groups * groups), jnp.int32),
            pltpu.VMEM((owners, LANES), jnp.float32),
            pltpu.SemaphoreType.DMA(()),
            pltpu.SemaphoreType.DMA((4,)),
        ],
        compiler_params=pltpu.CompilerParams(vmem_limit_bytes=24 << 20),
        cost_estimate=pl.CostEstimate(
            flops=rows * rows * EXT3, bytes_accessed=2 * rows * EXT3, transcendentals=0
        ),
    )(
        *in_hbm(pair_groups, owner.reshape(1, pairs), owner_slot.reshape(1, pairs)),
        potential,
        near,
        *in_hbm(basis),
    )


def integrated_far(far, near_total, potential, places, slots, capacity):
    rows = far.shape[0]
    groups = rows // BASIS
    vmem, hbm = pl.BlockSpec(memory_space=pltpu.VMEM), pl.BlockSpec(memory_space=pltpu.HBM)
    return pl.pallas_call(
        functools.partial(far_kernel, groups),
        name="integrate_far",
        out_shape=jax.ShapeDtypeStruct(
            (slots.shape[0], capacity * BASIS // 2 + slots.shape[1], LANES), jnp.bfloat16
        ),
        in_specs=[hbm, vmem, vmem, vmem, vmem],
        out_specs=hbm,
        scratch_shapes=[
            pltpu.VMEM((rows, padded(rows)), jnp.float32),
            pltpu.VMEM((groups * groups, BASIS // 2, LANES), jnp.bfloat16),
            pltpu.SMEM(places.shape, jnp.int32),
            pltpu.SemaphoreType.DMA((2,)),
            pltpu.SemaphoreType.DMA(()),
        ],
        compiler_params=pltpu.CompilerParams(vmem_limit_bytes=24 << 20),
        cost_estimate=pl.CostEstimate(
            flops=rows * rows * EXT3, bytes_accessed=2 * rows * EXT3, transcendentals=0
        ),
    )(places, slots, potential, far, near_total)


def store_kernel(capacity, got, store, total, other, packed, written):
    lines = BASIS // 2
    pitch = lines + 1
    stored = store.shape[0]
    total[...] = jnp.zeros_like(total)
    other[...] = jnp.zeros_like(other)
    for s in range(got.shape[0]):
        slots = got[s, capacity * lines : capacity * lines + 8, :].astype(jnp.float32)
        slots = slots[:1].astype(jnp.int32)
        for r in range(capacity):
            at = pl.ds(slots[0, r] * pitch, lines)
            sums = (total, other)[r % 2]
            sums[at, :] += got[s, r * lines : (r + 1) * lines, :].astype(jnp.float32)
    in_low = lax.broadcasted_iota(jnp.int32, (stored, LANES), 1) < BASIS
    pieces = 4
    span = lines // 2 // pieces
    copies = []
    for piece in range(pieces):
        for i in range(piece * span, (piece + 1) * span):
            even, odd = [
                total[pl.ds(line, stored, stride=pitch), :]
                + other[pl.ds(line, stored, stride=pitch), :]
                for line in (2 * i, 2 * i + 1)
            ]
            for j, row in (
                (i, jnp.where(in_low, even, pltpu.roll(odd, BASIS, axis=1))),
                (i + lines // 2, jnp.where(in_low, pltpu.roll(even, BASIS, axis=1), odd)),
            ):
                packed[:, j * LANES : (j + 1) * LANES] = row.astype(packed.dtype)
        for half in range(2):
            columns = pl.ds((half * lines // 2 + piece * span) * LANES, span * LANES)
            copies.append(
                pltpu.make_async_copy(
                    packed.at[:, columns], store.at[:, columns], written.at[len(copies)]
                )
            )
            copies[-1].start()
    for copy in copies:
        copy.wait()


def stored_blocks(got, rows, capacity):
    vmem, hbm = pl.BlockSpec(memory_space=pltpu.VMEM), pl.BlockSpec(memory_space=pltpu.HBM)
    return pl.pallas_call(
        functools.partial(store_kernel, capacity),
        name="store",
        out_shape=jax.ShapeDtypeStruct((rows, BASIS * BASIS), jnp.bfloat16),
        in_specs=[vmem],
        out_specs=hbm,
        scratch_shapes=[
            pltpu.VMEM(((rows + 1) * (BASIS // 2 + 1) + 7, LANES), jnp.float32),
            pltpu.VMEM(((rows + 1) * (BASIS // 2 + 1) + 7, LANES), jnp.float32),
            pltpu.VMEM((rows, BASIS * BASIS), jnp.bfloat16),
            pltpu.SemaphoreType.DMA((8,)),
        ],
        compiler_params=pltpu.CompilerParams(vmem_limit_bytes=24 << 20),
        cost_estimate=pl.CostEstimate(
            flops=got.size, bytes_accessed=2 * got.size, transcendentals=0
        ),
    )(got)


def per_device(basis, density_blocks, pair_groups, owner, owner_slot):
    pairs = density_blocks.shape[0]
    owners = lax.axis_size("gx") * lax.axis_size("gy")
    capacity = max(2, 2 * pairs // owners)
    groups = basis.shape[0]
    basis = basis.reshape(groups * BASIS, EXT3)
    box, swapped, near_table = collocated(basis, density_blocks, pair_groups)
    box = merged_z(box, swapped, "gz")
    box = jnp.stack(merged(box[0], box[1], "gy"))
    odd, near, far = merged_halves(box[:, : EXT // 2], box[:, EXT // 2 :], "gx")
    near, far = slater_potential(near), slater_potential(far)

    total, far_table, places, slots = integrated_near(
        near_table, basis, near, pair_groups, owner, owner_slot, owners
    )
    send = integrated_far(far_table, total, far, places, slots, capacity)
    got = lax.all_to_all(send, ("gx", "gy"), split_axis=0, concat_axis=0, tiled=True)

    potential = jnp.concatenate(
        [jnp.where(odd, near, far)[:, RIM:], jnp.where(odd, far, near)[:, :RIM]], axis=1
    ).reshape(2, CELLS, EXT // 2, EXT)[..., RIM : RIM + CELLS]
    potential = jnp.concatenate([potential[0, :, RIM:], potential[1, :, :RIM]], axis=1)
    return stored_blocks(got, pairs, capacity), potential


def solution(mesh):
    return jax.shard_map(
        per_device,
        mesh=mesh,
        in_specs=(
            P(("gx", "gy", "gz"), None, None),
            P(("gx", "gy", "gz"), None),
            P(None, ("gx", "gy", "gz")),
            P(("gx", "gy", "gz"), None),
            P(("gx", "gy", "gz")),
        ),
        out_specs=(P(("gx", "gy", "gz"), None), P("gx", "gy", "gz")),
        check_vma=False,
    )
```

```python
import functools

import jax
import jax.numpy as jnp
from jax import lax
from jax.experimental import pallas as pl
from jax.experimental.pallas import tpu as pltpu
from jax.sharding import PartitionSpec as P

BASIS = 64
CELLS = 8
RIM = 4
EXT = 16
EXT3 = 4096
LANES = 128

XC_COEF = 0.9847450218426965
GRID_WEIGHT = 0.015625


def slater_potential(density):
    return -XC_COEF * density / jnp.cbrt(density * density + 1.0)


def neighbour_swaps(count, first):
    pairs = []
    for low in range(first, count + first, 2):
        left, right = low % count, (low + 1) % count
        pairs += [(left, right), (right, left)]
    return pairs


def merged_halves(low, high, axis):
    count = lax.axis_size(axis)
    odd = lax.axis_index(axis) % 2 == 1
    near, far = jnp.where(odd, low, high), jnp.where(odd, high, low)
    near = near + lax.ppermute(near, axis, neighbour_swaps(count, 0))
    far = far + lax.ppermute(far, axis, neighbour_swaps(count, 1))
    return odd, near, far


def merged(low, high, axis):
    odd, near, far = merged_halves(low, high, axis)
    return jnp.where(odd, near, far), jnp.where(odd, far, near)


def merged_z(box, swapped, axis):
    count = lax.axis_size(axis)
    if count == 2:
        return box + lax.ppermute(swapped, axis, neighbour_swaps(count, 0))
    odd = lax.axis_index(axis) % 2 == 1
    lane = lax.broadcasted_iota(jnp.int32, box.shape, box.ndim - 1)
    in_high = lane % EXT >= EXT // 2
    first = lax.ppermute(swapped, axis, neighbour_swaps(count, 0))
    second = lax.ppermute(swapped, axis, neighbour_swaps(count, 1))
    return box + jnp.where(in_high != odd, first, second)


def halves():
    odd = lax.axis_index("gx") % 2
    return (1 - odd) * (EXT3 // 2), odd * (EXT3 // 2)


def collocate_kernel(
    groups, pair_groups, blocks, basis, box, swapped, near,
    far, codes, local, spread, matrix, owner_of, arrived, staged,
):
    pairs = blocks.shape[0]
    pitch = BASIS + 1
    codes_copy = pltpu.make_async_copy(pair_groups, codes, staged.at[0])
    blocks_copy = pltpu.make_async_copy(blocks, local, staged.at[1])
    ahead, planes = 2, 4
    cells = planes * EXT * EXT
    copies, plane_of = [], []
    for begin, half in zip(halves(), (near, far)):
        for c in range(half.shape[1] // cells):
            first = pl.multiple_of(begin + c * cells, LANES)
            place = half.at[:, pl.ds(c * cells, cells)]
            copies.append(
                (
                    pltpu.make_async_copy(
                        basis.at[:, pl.ds(first, cells)], place, arrived.at[len(copies)]
                    ),
                    place,
                )
            )
            plane_of.append(begin // (EXT * EXT) + c * planes)
    for copy in [codes_copy, blocks_copy] + [copy for copy, _ in copies[:ahead]]:
        copy.start()
    spread[pl.ds(pairs * pitch, BASIS), :] = jnp.zeros((BASIS, LANES), jnp.float32)
    codes_copy.wait()
    for code in range(groups * groups):
        owner_of[code] = pairs
    for p in range(pairs):
        owner_of[codes[0, p] * groups + codes[1, p]] = p
    blocks_copy.wait()
    in_low = lax.broadcasted_iota(jnp.int32, (pairs, LANES), 1) < BASIS
    for j in range(BASIS // 2):
        two_rows = local[:, j * LANES : (j + 1) * LANES].astype(jnp.float32)
        turned = pltpu.roll(two_rows, BASIS, axis=1)
        spread[pl.ds(2 * j, pairs, stride=pitch), :] = jnp.where(in_low, two_rows, turned)
        spread[pl.ds(2 * j + 1, pairs, stride=pitch), :] = jnp.where(in_low, turned, two_rows)
    left = lax.broadcasted_iota(jnp.int32, (BASIS, LANES), 1) < BASIS
    for first in range(groups):
        for second in range(0, groups, 2):
            code = first * groups + second
            block = spread[pl.ds(owner_of[code] * pitch, BASIS), :]
            if second + 1 < groups:
                block = jnp.where(left, block, spread[pl.ds(owner_of[code + 1] * pitch, BASIS), :])
            matrix[
                first * BASIS : (first + 1) * BASIS, second * BASIS : second * BASIS + LANES
            ] = block.astype(matrix.dtype)
    dense = matrix[:, : groups * BASIS]
    for c, (copy, place) in enumerate(copies):
        copy.wait()
        if c + ahead < len(copies):
            copies[c + ahead][0].start()
        values = place[...]
        projected = jnp.dot(dense, values, preferred_element_type=jnp.float32)
        summed = jnp.sum(values.astype(jnp.float32) * projected, axis=0, keepdims=True)
        for t in range(summed.shape[1] // LANES):
            box[t % 2, pl.ds(plane_of[c] + t // 2, 1), :] = summed[:, t * LANES : (t + 1) * LANES]
    lane = lax.broadcasted_iota(jnp.int32, (EXT, LANES), 1)
    for half in range(2):
        cells = box[half]
        swapped[half] = jnp.where(
            lane % EXT < EXT // 2,
            pltpu.roll(cells, LANES - EXT // 2, axis=1),
            pltpu.roll(cells, EXT // 2, axis=1),
        )


def collocated(basis, density_blocks, pair_groups):
    rows, pairs = basis.shape[0], density_blocks.shape[0]
    groups = rows // BASIS
    vmem, hbm = pl.BlockSpec(memory_space=pltpu.VMEM), pl.BlockSpec(memory_space=pltpu.HBM)
    return pl.pallas_call(
        functools.partial(collocate_kernel, groups),
        name="collocate",
        out_shape=(
            jax.ShapeDtypeStruct((2, EXT, LANES), jnp.float32),
            jax.ShapeDtypeStruct((2, EXT, LANES), jnp.float32),
            jax.ShapeDtypeStruct((rows, EXT3 // 2), basis.dtype),
        ),
        in_specs=[hbm, hbm, hbm],
        out_specs=[vmem, vmem, vmem],
        scratch_shapes=[
            pltpu.VMEM((rows, EXT3 // 2), basis.dtype),
            pltpu.SMEM(pair_groups.shape, jnp.int32),
            pltpu.VMEM(density_blocks.shape, density_blocks.dtype),
            pltpu.VMEM(((pairs + 1) * (BASIS + 1) + 7, LANES), jnp.float32),
            pltpu.VMEM((rows, padded(rows)), jnp.bfloat16),
            pltpu.SMEM((groups * groups,), jnp.int32),
            pltpu.SemaphoreType.DMA((EXT // 2,)),
            pltpu.SemaphoreType.DMA((2,)),
        ],
        compiler_params=pltpu.CompilerParams(vmem_limit_bytes=24 << 20),
        cost_estimate=pl.CostEstimate(
            flops=2 * rows * rows * EXT3, bytes_accessed=2 * rows * EXT3, transcendentals=0
        ),
    )(*in_hbm(pair_groups, density_blocks, basis))


def tabulate(groups, span, codes, owner, slot, counts, place, slot_rows):
    pairs, owners = codes.shape[1], counts.shape[0]
    lines = BASIS // 2
    slot_rows[...] = jnp.full(slot_rows.shape, pairs, jnp.float32)
    lane = lax.broadcasted_iota(jnp.int32, (1, LANES), 1)
    for o in range(owners):
        counts[o] = 0
    for code in range(groups * groups):
        place[0, code] = -1
    for p in range(pairs):
        o = owner[0, p]
        rank = counts[o]
        counts[o] = rank + 1
        code = codes[0, p] * groups + codes[1, p]
        place[0, code] = o * span + rank * lines
        row = slot_rows[pl.ds(o, 1), :]
        slot_rows[pl.ds(o, 1), :] = jnp.where(lane == rank, slot[0, p].astype(jnp.float32), row)
    free_owner, free_rank = jnp.int32(0), counts[0]
    for o in range(1, owners):
        fewer = counts[o] < free_rank
        free_owner = jnp.where(fewer, o, free_owner)
        free_rank = jnp.where(fewer, counts[o], free_rank)
    free_row = free_owner * span + free_rank * lines
    for code in range(groups * groups):
        row = place[0, code]
        place[0, code] = jnp.where(row < 0, free_row, row)


def overlaps(table, potential, planes=4):
    cells = planes * EXT * EXT
    for c in range(table.shape[1] // cells):
        values = table[:, c * cells : (c + 1) * cells]
        weight = jnp.concatenate(
            [
                potential[t % 2, planes * c + t // 2 : planes * c + t // 2 + 1, :]
                for t in range(cells // LANES)
            ],
            axis=1,
        )
        weighted = (values.astype(jnp.float32) * weight).astype(jnp.bfloat16)
        yield lax.dot_general(
            weighted, values, (((1,), (1,)), ((), ())), preferred_element_type=jnp.float32
        )


def near_kernel(
    groups, span, pair_groups, owner, owner_slot, potential, near, basis, total, far, places, slots,
    codes, owners_of, slots_of, counts, place, slot_rows, arrived, staged,
):
    rows = near.shape[0]
    begin = pl.multiple_of(halves()[1], LANES)
    far_copy = pltpu.make_async_copy(basis.at[:, pl.ds(begin, far.shape[1])], far, arrived)
    tables = [
        pltpu.make_async_copy(source, target, staged.at[i])
        for i, (source, target) in enumerate(
            [(pair_groups, codes), (owner, owners_of), (owner_slot, slots_of)]
        )
    ]
    for copy in tables + [far_copy]:
        copy.start()
    for c, part in enumerate(overlaps(near, potential)):
        if c == 0:
            total[:, :rows] = part
            for copy in tables:
                copy.wait()
            tabulate(groups, span, codes, owners_of, slots_of, counts, place, slot_rows)
        else:
            total[:, :rows] += part
    places_copy = pltpu.make_async_copy(place, places, staged.at[3])
    places_copy.start()
    for o in range(slots.shape[0]):
        slots[o] = jnp.broadcast_to(slot_rows[o : o + 1, :], slots.shape[1:]).astype(slots.dtype)
    places_copy.wait()
    far_copy.wait()


def far_kernel(
    groups, places, slots, potential, far, near_total, send, total, blocks, place, staged, sent
):
    rows = groups * BASIS
    lines = BASIS // 2
    places_copy = pltpu.make_async_copy(places, place, staged.at[0])
    places_copy.start()
    span = send.shape[0] // slots.shape[0]
    for o in range(slots.shape[0]):
        rows_of = pl.ds((o + 1) * span - slots.shape[1], slots.shape[1])
        pltpu.make_async_copy(slots.at[o], send.at[rows_of, :], staged.at[1]).start()
    for c, part in enumerate(overlaps(far, potential)):
        if c == 0:
            total[:, :rows] = near_total[:, :rows] + part
        else:
            total[:, :rows] += part
    places_copy.wait()
    left = lax.broadcasted_iota(jnp.int32, (lines, LANES), 1) < BASIS
    for first in range(groups):
        for second in range(groups):
            code = first * groups + second
            begin = second // 2 * LANES
            upper = total[first * BASIS : first * BASIS + lines, begin : begin + LANES]
            lower = total[first * BASIS + lines : (first + 1) * BASIS, begin : begin + LANES]
            if second % 2 == 0:
                lower = pltpu.roll(lower, BASIS, axis=1)
            else:
                upper = pltpu.roll(upper, BASIS, axis=1)
            blocks[code] = (jnp.where(left, upper, lower) * GRID_WEIGHT).astype(blocks.dtype)
            row = pl.multiple_of(place[0, code], 8)
            pltpu.make_async_copy(
                blocks.at[code], send.at[pl.ds(row, lines), :], sent
            ).start()
    pltpu.make_async_copy(slots, slots, staged.at[1]).wait()
    pltpu.make_async_copy(blocks, blocks, sent).wait()


def in_hbm(*arrays):
    return [pltpu.with_memory_space_constraint(x, pltpu.HBM) for x in arrays]


def padded(rows):
    return -(-rows // LANES) * LANES


def integrated_near(near, basis, potential, pair_groups, owner, owner_slot, owners, capacity):
    rows, pairs = basis.shape[0], pair_groups.shape[1]
    groups = rows // BASIS
    vmem, hbm = pl.BlockSpec(memory_space=pltpu.VMEM), pl.BlockSpec(memory_space=pltpu.HBM)
    return pl.pallas_call(
        functools.partial(near_kernel, groups, capacity * BASIS // 2 + 8),
        name="integrate_near",
        out_shape=(
            jax.ShapeDtypeStruct((rows, padded(rows)), jnp.float32),
            jax.ShapeDtypeStruct((rows, EXT3 // 2), basis.dtype),
            jax.ShapeDtypeStruct((1, groups * groups), jnp.int32),
            jax.ShapeDtypeStruct((owners, 8, LANES), jnp.bfloat16),
        ),
        in_specs=[hbm, hbm, hbm, vmem, vmem, hbm],
        out_specs=[vmem, vmem, hbm, vmem],
        scratch_shapes=[
            pltpu.SMEM((2, pairs), jnp.int32),
            pltpu.SMEM((1, pairs), jnp.int32),
            pltpu.SMEM((1, pairs), jnp.int32),
            pltpu.SMEM((owners,), jnp.int32),
            pltpu.SMEM((1, groups * groups), jnp.int32),
            pltpu.VMEM((owners, LANES), jnp.float32),
            pltpu.SemaphoreType.DMA(()),
            pltpu.SemaphoreType.DMA((4,)),
        ],
        compiler_params=pltpu.CompilerParams(vmem_limit_bytes=24 << 20),
        cost_estimate=pl.CostEstimate(
            flops=rows * rows * EXT3, bytes_accessed=2 * rows * EXT3, transcendentals=0
        ),
    )(
        *in_hbm(pair_groups, owner.reshape(1, pairs), owner_slot.reshape(1, pairs)),
        potential,
        near,
        *in_hbm(basis),
    )


def integrated_far(far, near_total, potential, places, slots, capacity):
    rows = far.shape[0]
    groups = rows // BASIS
    vmem, hbm = pl.BlockSpec(memory_space=pltpu.VMEM), pl.BlockSpec(memory_space=pltpu.HBM)
    return pl.pallas_call(
        functools.partial(far_kernel, groups),
        name="integrate_far",
        out_shape=jax.ShapeDtypeStruct(
            (slots.shape[0] * (capacity * BASIS // 2 + slots.shape[1]), LANES), jnp.bfloat16
        ),
        in_specs=[hbm, vmem, vmem, vmem, vmem],
        out_specs=hbm,
        scratch_shapes=[
            pltpu.VMEM((rows, padded(rows)), jnp.float32),
            pltpu.VMEM((groups * groups, BASIS // 2, LANES), jnp.bfloat16),
            pltpu.SMEM(places.shape, jnp.int32),
            pltpu.SemaphoreType.DMA((2,)),
            pltpu.SemaphoreType.DMA(()),
        ],
        compiler_params=pltpu.CompilerParams(vmem_limit_bytes=24 << 20),
        cost_estimate=pl.CostEstimate(
            flops=rows * rows * EXT3, bytes_accessed=2 * rows * EXT3, transcendentals=0
        ),
    )(places, slots, potential, far, near_total)


def store_kernel(capacity, got, store, total, other, packed, written):
    lines = BASIS // 2
    pitch = lines + 1
    stored = store.shape[0]
    total[...] = jnp.zeros_like(total)
    other[...] = jnp.zeros_like(other)
    for s in range(got.shape[0]):
        slots = got[s, capacity * lines : capacity * lines + 8, :].astype(jnp.float32)
        slots = slots[:1].astype(jnp.int32)
        for r in range(capacity):
            at = pl.ds(slots[0, r] * pitch, lines)
            sums = (total, other)[r % 2]
            sums[at, :] += got[s, r * lines : (r + 1) * lines, :].astype(jnp.float32)
    in_low = lax.broadcasted_iota(jnp.int32, (stored, LANES), 1) < BASIS
    pieces = 4
    span = lines // 2 // pieces
    copies = []
    for piece in range(pieces):
        for i in range(piece * span, (piece + 1) * span):
            even, odd = [
                total[pl.ds(line, stored, stride=pitch), :]
                + other[pl.ds(line, stored, stride=pitch), :]
                for line in (2 * i, 2 * i + 1)
            ]
            for j, row in (
                (i, jnp.where(in_low, even, pltpu.roll(odd, BASIS, axis=1))),
                (i + lines // 2, jnp.where(in_low, pltpu.roll(even, BASIS, axis=1), odd)),
            ):
                packed[:, j * LANES : (j + 1) * LANES] = row.astype(packed.dtype)
        for half in range(2):
            columns = pl.ds((half * lines // 2 + piece * span) * LANES, span * LANES)
            copies.append(
                pltpu.make_async_copy(
                    packed.at[:, columns], store.at[:, columns], written.at[len(copies)]
                )
            )
            copies[-1].start()
    for copy in copies:
        copy.wait()


def stored_blocks(got, rows, capacity):
    vmem, hbm = pl.BlockSpec(memory_space=pltpu.VMEM), pl.BlockSpec(memory_space=pltpu.HBM)
    return pl.pallas_call(
        functools.partial(store_kernel, capacity),
        name="store",
        out_shape=jax.ShapeDtypeStruct((rows, BASIS * BASIS), jnp.bfloat16),
        in_specs=[vmem],
        out_specs=hbm,
        scratch_shapes=[
            pltpu.VMEM(((rows + 1) * (BASIS // 2 + 1) + 7, LANES), jnp.float32),
            pltpu.VMEM(((rows + 1) * (BASIS // 2 + 1) + 7, LANES), jnp.float32),
            pltpu.VMEM((rows, BASIS * BASIS), jnp.bfloat16),
            pltpu.SemaphoreType.DMA((8,)),
        ],
        compiler_params=pltpu.CompilerParams(vmem_limit_bytes=24 << 20),
        cost_estimate=pl.CostEstimate(
            flops=got.size, bytes_accessed=2 * got.size, transcendentals=0
        ),
    )(got)


def per_device(basis, density_blocks, pair_groups, owner, owner_slot):
    pairs = density_blocks.shape[0]
    owners = lax.axis_size("gx") * lax.axis_size("gy")
    capacity = max(2, 2 * pairs // owners)
    groups = basis.shape[0]
    basis = basis.reshape(groups * BASIS, EXT3)
    box, swapped, near_table = collocated(basis, density_blocks, pair_groups)
    box = merged_z(box, swapped, "gz")
    box = jnp.stack(merged(box[0], box[1], "gy"))
    odd, near, far = merged_halves(box[:, : EXT // 2], box[:, EXT // 2 :], "gx")
    near, far = slater_potential(near), slater_potential(far)

    total, far_table, places, slots = integrated_near(
        near_table, basis, near, pair_groups, owner, owner_slot, owners, capacity
    )
    send = integrated_far(far_table, total, far, places, slots, capacity)
    send = send.reshape(owners, -1, LANES)
    got = lax.all_to_all(send, ("gx", "gy"), split_axis=0, concat_axis=0, tiled=True)

    potential = jnp.concatenate(
        [jnp.where(odd, near, far)[:, RIM:], jnp.where(odd, far, near)[:, :RIM]], axis=1
    ).reshape(2, CELLS, EXT // 2, EXT)[..., RIM : RIM + CELLS]
    potential = jnp.concatenate([potential[0, :, RIM:], potential[1, :, :RIM]], axis=1)
    return stored_blocks(got, pairs, capacity), potential


def solution(mesh):
    return jax.shard_map(
        per_device,
        mesh=mesh,
        in_specs=(
            P(("gx", "gy", "gz"), None, None),
            P(("gx", "gy", "gz"), None),
            P(None, ("gx", "gy", "gz")),
            P(("gx", "gy", "gz"), None),
            P(("gx", "gy", "gz")),
        ),
        out_specs=(P(("gx", "gy", "gz"), None), P("gx", "gy", "gz")),
        check_vma=False,
    )
```
